256 devices in a mesh: dp: 32 (over z, y), tensor: 8 (over x, core).
Axes of the slice: x: 4, y: 4, z: 8, core: 2. Of those that a mesh axis runs over, the one named last changes fastest.
Arguments:
- inputs: bfloat16 [16384, 4096], P('dp'), may hold values from -6 to 6
- weight: bfloat16 [4096, 4096], P(None, 'tensor'), may hold values from -0.09375 to 0.09375
- targets: bfloat16 [16384, 4096], P('dp', 'tensor'), may hold values from -6 to 6
- momentum: float32 [4096, 4096], P('dp', 'tensor'), may hold values from -6 to 6
Outputs:
- input_grad: bfloat16 [4096, 16384], P('tensor', 'dp')
- new_momentum: float32 [4096, 4096], P('dp', 'tensor')
- tree_norms: float32 [2], replicated
The draws below stay inside these ranges and needn't reach their ends.
All inputs are finite; a program needn't handle non-finite values.
Results may differ from the reference program's by a relative error of at most 0.013.
Values may be sent and summed in bfloat16 or wider, within the bound.
A program may use at most 128 MiB of HBM per device.

```python
import math
import jax
import jax.numpy as jnp
from jax import lax

D = 4096
ROWS = 512
TOTAL_ROWS = 16384
N_DP = 32
N_TENSOR = 8


def block_levels(stream_key, shape, cuts, least, top_value):
    factor_of, own = 1.0, jax.random.fold_in(stream_key, 6)
    for axis_at, blocks in cuts:
        steps = jnp.exp(jax.random.uniform(jax.random.fold_in(own, axis_at), (blocks,), jnp.float32, least / len(cuts), top_value / len(cuts)))
        factor_of = factor_of * jnp.repeat(steps, shape[axis_at] // blocks).reshape([-1 if axis == axis_at else 1 for axis in range(len(shape))])
    return factor_of


def normal_values(key, extent, scale, bound, cuts=(), dtype=jnp.bfloat16):
    gain = block_levels(key, extent, cuts, -0.22, 0.18) if cuts else 1.0
    result = jax.random.normal(key, extent, jnp.float32) * scale * gain
    return jnp.minimum(jnp.maximum(result, -bound), bound).astype(dtype)


def setup_inputs(seed: int = 0) -> dict:
    arg_keys = jax.random.split(jax.random.key(seed), 5)
    inputs = normal_values(arg_keys[0], (TOTAL_ROWS, D), 1.0, 6.0, ((0, 32),))
    weight = normal_values(arg_keys[1], (D, D), D ** -0.5, 0.09375, ((1, 8),))
    targets = normal_values(arg_keys[2], (TOTAL_ROWS, D), 1.0, 6.0, ((0, 32), (1, 8)))
    momentum = normal_values(arg_keys[3], (D, D), 1.0, 6.0, ((0, 32), (1, 8)), jnp.float32)
    return dict(inputs=inputs, weight=weight, targets=targets, momentum=momentum)


def group_terms(inputs_g, targets_g, weight):
    outputs = jnp.dot(inputs_g, weight, preferred_element_type=jnp.float32)
    error = (outputs - targets_g.astype(jnp.float32)).astype(jnp.bfloat16)
    grad = lax.dot_general(inputs_g, error, (((0,), (0,)), ((), ())), preferred_element_type=jnp.float32)
    grad = grad * (1.0 / math.sqrt(ROWS))
    width = D // N_TENSOR
    total = jnp.zeros((D, inputs_g.shape[0]), jnp.float32)
    for block in range(N_TENSOR):
        part = lax.dot_general(weight[:, block * width:(block + 1) * width], error[:, block * width:(block + 1) * width], (((1,), (1,)), ((), ())), preferred_element_type=jnp.float32)
        total = total + part.astype(jnp.bfloat16).astype(jnp.float32)
    return (grad, total.astype(jnp.bfloat16))

def adasum_norms(first, second):
    cross = jnp.sum(first * second)
    first_sq = jnp.sum(first * first)
    second_sq = jnp.sum(second * second)
    merged = (1.0 - cross / (2.0 * first_sq)) * first + (1.0 - cross / (2.0 * second_sq)) * second
    return (merged, first_sq, second_sq)

def reference(inputs, weight, targets, momentum):
    pieces = []

    def combine(lower, count):
        if count == 1:
            grad, partial_grad = group_terms(inputs[lower * ROWS:(lower + 1) * ROWS], targets[lower * ROWS:(lower + 1) * ROWS], weight)
            pieces.append((lower, partial_grad))
            return grad
        half = count // 2
        first = combine(lower, half)
        second = combine(lower + half, half)
        return adasum_norms(first, second)[0]
    half_all = N_DP // 2
    first_all = combine(0, half_all)
    second_all = combine(half_all, half_all)
    combined, first_sq, second_sq = adasum_norms(first_all, second_all)
    ordered = sorted(pieces, key=lambda item: item[0])
    input_grad = jnp.concatenate([item[1] for item in ordered], axis=1)
    tree_norms = jnp.sqrt(jnp.stack([first_sq, second_sq])) / D
    return (input_grad, 0.9 * momentum + combined, tree_norms)
```

```python
import math

import jax
import jax.numpy as jnp
from jax import lax
from jax.sharding import PartitionSpec as P

ROWS = 512
HI = lax.Precision.HIGHEST


def tree_weights(gram):
    count = gram.shape[0]
    items = jnp.eye(count, dtype=jnp.float32)
    while items.shape[0] > 1:
        first, second = items[0::2], items[1::2]
        first_g = jnp.dot(first, gram, precision=HI)
        second_g = jnp.dot(second, gram, precision=HI)
        cross = jnp.sum(first_g * second, axis=1)
        first_sq = jnp.sum(first_g * first, axis=1)
        second_sq = jnp.sum(second_g * second, axis=1)
        items = (1.0 - cross / (2.0 * first_sq))[:, None] * first + (
            1.0 - cross / (2.0 * second_sq)
        )[:, None] * second
    return items[0], jnp.concatenate([first_sq, second_sq])


def body(inputs, weight, targets, momentum):
    outputs = jnp.dot(inputs, weight, preferred_element_type=jnp.float32)
    error = (outputs - targets.astype(jnp.float32)).astype(jnp.bfloat16)
    summed = lax.psum_scatter(
        lax.dot_general(
            weight, error, (((1,), (1,)), ((), ())), preferred_element_type=jnp.float32
        ).astype(jnp.bfloat16),
        "tensor",
        scatter_dimension=0,
        tiled=True,
    )
    grad = lax.dot_general(
        inputs, error, (((0,), (0,)), ((), ())), preferred_element_type=jnp.float32
    )
    grad = (grad * (1.0 / math.sqrt(ROWS))).astype(jnp.bfloat16)
    groups = lax.axis_size("dp")
    block_rows = grad.shape[0] // groups
    columns = grad.shape[1]
    pieces = lax.all_to_all(
        grad.reshape(groups, block_rows, columns), "dp", split_axis=0, concat_axis=0
    )
    partial = jnp.einsum("gij,hij->gh", pieces, pieces, preferred_element_type=jnp.float32)
    gram = lax.psum(partial, ("dp", "tensor"))
    weights, squares = tree_weights(gram)
    combined = jnp.sum(weights[:, None, None] * pieces.astype(jnp.float32), axis=0)
    tree_norms = jnp.sqrt(squares) / weight.shape[0]
    return (summed, 0.9 * momentum + combined, tree_norms)


def solution(mesh):
    return jax.shard_map(
        body,
        mesh=mesh,
        in_specs=(P("dp", None), P(None, "tensor"), P("dp", "tensor"), P("dp", "tensor")),
        out_specs=(P("tensor", "dp"), P("dp", "tensor"), P()),
        check_vma=False,
    )
```

```python
import functools
import math

import jax
import jax.numpy as jnp
from jax import lax
from jax.experimental import pallas as pl
from jax.experimental.pallas import tpu as pltpu
from jax.sharding import PartitionSpec as P

MESH = pl.DeviceIdType.MESH
NZ, NY, NX, NC = 8, 4, 4, 2
NT = NX * NC
F32, BF16 = jnp.float32, jnp.bfloat16
KCHUNKS = 4
YPAIRS = [(i, j) for i in range(NY) for j in range(i, NY)]
ZPAIRS = [(i, j) for i in range(NZ) for j in range(i, NZ)]


def tree(gram, pairs):
    count = max(j for _, j in pairs) + 1
    value = {}
    for at, (i, j) in enumerate(pairs):
        value[i, j] = value[j, i] = gram[at]
    items = [{i: None} for i in range(count)]

    def weighted(term, coefficient):
        return term if coefficient is None else term * coefficient

    def inner(first, second):
        total = None
        for i, a in first.items():
            for j, c in second.items():
                term = weighted(weighted(value[i, j], a), c)
                total = term if total is None else total + term
        return total

    while len(items) > 1:
        merged = []
        for at in range(0, len(items), 2):
            first, second = items[at], items[at + 1]
            cross, first_sq, second_sq = inner(first, second), inner(first, first), inner(second, second)
            left = 1.0 - cross / (2.0 * first_sq)
            right = 1.0 - cross / (2.0 * second_sq)
            item = {i: weighted(left, a) for i, a in first.items()}
            item.update({i: weighted(right, c) for i, c in second.items()})
            merged.append(item)
        items = merged
    return [items[0][i] for i in range(count)], first_sq, second_sq


def kernel(
    inputs, weight, targets,
    ig_out, comb_out, norm_out,
    xin, w, tg, acc, gin, et, psend, precv, ppart, xrecv, gbuf, zsend, zrecv,
    gsum, yred, tred, zred, mine,
    ld_sem, own_sem, iy_send, iy_recv, ix_send, ix_recv, is_send, is_recv,
    e_send, e_recv, p_send, p_recv, q_send, q_recv, z_send, z_recv, r_send, r_recv,
):
    dp, t = lax.axis_index("dp"), lax.axis_index("tensor")
    z, y, x, c = dp // NY, dp % NY, t // NC, t % NC
    rows, width = inputs.shape
    cols = weight.shape[1]
    kc = width // KCHUNKS
    part_rows = rows // NT
    block = width // (NZ * NY)
    wide = block * NZ

    def at(dz=0, dy=0, dt=None):
        return ((z + dz) % NZ * NY + (y + dy) % NY, t if dt is None else (t + dt) % NT)

    def at_x(dx, core):
        return (dp, (x + dx) % NX * NC + core)

    loads = []
    for i in range(KCHUNKS):
        a = pltpu.make_async_copy(inputs.at[:, i * kc:(i + 1) * kc], xin.at[:, i * kc:(i + 1) * kc], ld_sem.at[2 * i])
        b = pltpu.make_async_copy(weight.at[i * kc:(i + 1) * kc], w.at[i * kc:(i + 1) * kc], ld_sem.at[2 * i + 1])
        a.start()
        b.start()
        loads.append((a, b))
    tg_load = pltpu.make_async_copy(targets, tg, ld_sem.at[2 * KCHUNKS])
    tg_load.start()

    barrier = pltpu.get_barrier_semaphore()
    peers = [at(dz=k) for k in range(1, NZ)] + [at(dy=k) for k in range(1, NY)] + [at(dt=k) for k in range(1, NT)]
    for peer in peers:
        pl.semaphore_signal(barrier, inc=1, device_id=peer, device_id_type=MESH)
    pl.semaphore_wait(barrier, len(peers))

    def remote(src, dst, send, recv, peer):
        return pltpu.make_async_remote_copy(
            src_ref=src, dst_ref=dst, send_sem=send, recv_sem=recv, device_id=peer, device_id_type=MESH
        )

    my_rows = pl.ds(pl.multiple_of(t * part_rows, part_rows), part_rows)
    for k in (2, 1, 3):
        for b in range(NZ):
            col = pl.multiple_of((b * NY + (y + k) % NY) * block, block)
            remote(
                inputs.at[my_rows, pl.ds(col, block)], gin.at[y, my_rows, b * block:(b + 1) * block],
                iy_send.at[k - 1], iy_recv.at[3 - k], at(dy=k),
            ).start()
    for b in range(NZ):
        col = pl.multiple_of((b * NY + y) * block, block)
        pltpu.make_async_copy(inputs.at[:, pl.ds(col, block)], gin.at[y, :, b * block:(b + 1) * block], own_sem).start()

    for i, (a, b) in enumerate(loads):
        a.wait()
        b.wait()
        part = jnp.dot(xin[:, i * kc:(i + 1) * kc], w[i * kc:(i + 1) * kc, :], preferred_element_type=F32)
        if i == 0:
            acc[...] = part
        else:
            acc[...] += part
    tg_load.wait()
    et[y] = jnp.transpose((acc[...] - tg[...].astype(F32)).astype(BF16))

    half = cols // 2
    low, high = pl.ds(0, half), pl.ds(half, half)
    right, left, across = (y + 1) % NY, (y + 3) % NY, (y + 2) % NY

    def send_error(index, sem, part, dy):
        copy = remote(et.at[index, part], et.at[index, part], e_send.at[sem], e_recv.at[sem], at(dy=dy))
        copy.start()
        return copy

    e_copies = [
        send_error(y, 0, low, 3),
        send_error(y, 3, high, 1),
        send_error(y, 1, high, 3),
        send_error(y, 2, low, 1),
    ]

    def e_wait(index, sem, part):
        remote(et.at[index, part], et.at[index, part], e_send.at[sem], e_recv.at[sem], at(dy=1)).wait_recv()

    sib = at_x(0, 1 - c)
    for k in (1, 2, 3):
        remote(
            gin.at[(y + k) % NY, my_rows], gin.at[(y + k) % NY, my_rows], iy_send.at[k - 1], iy_recv.at[k - 1], at(dy=k)
        ).wait_recv()
    ix_copies, is_copies = [], []

    def share(rows_at, sends, recvs, base, peer, out):
        for k in (1, 2, 3):
            ref = gin.at[(y + k) % NY, rows_at]
            copy = remote(ref, ref, sends.at[base + k - 1], recvs.at[base + k - 1], peer)
            copy.start()
            out.append(copy)

    for j in (2, 1, 3):
        share(my_rows, ix_send, ix_recv, (3 - j) * 3, at_x(j, c), ix_copies)
    share(my_rows, is_send, is_recv, 0, sib, is_copies)

    p_copies = []
    for j in range(NX):
        start = pl.multiple_of(((x + j) % NX * NC + 1 - c) * cols, cols)
        psend[j] = jnp.dot(w[pl.ds(start, cols), :], et[y], preferred_element_type=F32).astype(BF16)
        copy = remote(psend.at[j], precv.at[j], p_send.at[j], p_recv.at[j], sib)
        copy.start()
        p_copies.append(copy)
    for j in range(NX):
        start = pl.multiple_of(((x + j) % NX * NC + c) * cols, cols)
        ppart[j] = jnp.dot(w[pl.ds(start, cols), :], et[y], preferred_element_type=F32).astype(BF16)

    def gradient(index):
        gbuf[index] = jnp.dot(et[index], gin[index], preferred_element_type=F32)

    pltpu.make_async_copy(gin.at[y], gin.at[y], own_sem).wait()
    gradient(y)

    e_wait(right, 0, low)
    e_copies.append(send_error(right, 4, low, 3))
    e_wait(left, 3, high)
    e_copies.append(send_error(left, 5, high, 1))

    for j in range(NX):
        p_copies[j].wait_recv()
        ppart[j] = (ppart[j].astype(F32) + precv[j].astype(F32)).astype(BF16)

    for j in (1, 3, 2):
        rows_at = pl.ds(pl.multiple_of(((x + j) % NX * NC + c) * part_rows, part_rows), part_rows)
        for k in (1, 2, 3):
            ref = gin.at[(y + k) % NY, rows_at]
            remote(ref, ref, ix_send.at[0], ix_recv.at[(j - 1) * 3 + k - 1], sib).wait_recv()
        share(rows_at, is_send, is_recv, j * 3, sib, is_copies)

    q_copies = []
    for j in (2, 1, 3):
        copy = remote(ppart.at[j], xrecv.at[3 - j], q_send.at[j - 1], q_recv.at[3 - j], at_x(j, c))
        copy.start()
        q_copies.append(copy)

    for copy in is_copies:
        copy.wait_recv()
    e_wait(right, 1, high)
    gradient(right)
    e_wait(left, 2, low)
    gradient(left)
    e_wait(across, 4, low)
    e_wait(across, 5, high)
    gradient(across)

    gsum[...] = jnp.zeros_like(gsum)
    ones = jnp.ones((8, 128), F32)
    lane = lax.broadcasted_iota(jnp.int32, (8, 128), 1)

    def to_lanes(sums):
        for p, value in enumerate(sums):
            gsum[p:p + 1, :] = jnp.sum(value, axis=0, keepdims=True)
        return lax.dot_general(
            ones, gsum[...], (((1,), (1,)), ((), ())), precision=lax.Precision.HIGHEST, preferred_element_type=F32
        )

    def reduce_stage(value, slot, buffer, count, me, peer_of):
        mine[slot] = value
        buffer[me] = value
        for k in range(1, count):
            remote(mine.at[slot], buffer.at[me], r_send.at[slot], r_recv.at[slot], peer_of(k)).start()
        some = buffer.at[0:count - 1]
        remote(some, some, r_send.at[slot], r_recv.at[slot], peer_of(1)).wait()
        total = buffer[0]
        for k in range(1, count):
            total = total + buffer[k]
        return total

    def pick(vec, count):
        return [
            jnp.sum(jnp.where(lane == p, vec, 0.0), axis=1, keepdims=True)[0:1, :] for p in range(count)
        ]

    def fold(value):
        total = value[:, 0:128]
        for l in range(1, value.shape[1] // 128):
            total = total + value[:, l * 128:(l + 1) * 128]
        return total

    def y_step(i, sums):
        at_rows = pl.ds(pl.multiple_of(i * 8, 8), 8)
        items = [gbuf[k, at_rows, :] for k in range(NY)]
        return tuple(s + fold(items[a] * items[b]) for s, (a, b) in zip(sums, YPAIRS))

    zero = jnp.zeros((8, 128), F32)
    vec = to_lanes(lax.fori_loop(0, cols // 8, y_step, (zero,) * len(YPAIRS)))
    vec = reduce_stage(vec, 0, yred.at[0], NY, y, lambda k: at(dy=k))
    vec = reduce_stage(vec, 1, tred.at[0], NT, t, lambda k: at(dt=k))
    weights, _, _ = tree(pick(vec, len(YPAIRS)), YPAIRS)
    weights = [v * (1.0 / math.sqrt(rows)) for v in weights]

    def combine(b):
        lanes = pl.ds(pl.multiple_of(b * block, block), block)
        total = weights[0] * gbuf[0, :, lanes]
        for k in range(1, NY):
            total = total + weights[k] * gbuf[k, :, lanes]
        return total.astype(BF16)

    z_copies = []
    for k in (4, 3, 5, 2, 6, 1, 7):
        b = (z + k) % NZ
        zsend[k - 1] = combine(b)
        copy = remote(zsend.at[k - 1], zrecv.at[z], z_send.at[k - 1], z_recv.at[NZ - 1 - k], at(dz=k))
        copy.start()
        z_copies.append(copy)
    zrecv[z] = combine(z)

    for copy in q_copies:
        copy.wait_recv()
    total = ppart[0].astype(F32)
    for j in range(NX - 1):
        total = total + xrecv[j].astype(F32)
    ig_out[...] = total.astype(BF16)

    for k in range(1, NZ):
        remote(zrecv.at[(z + k) % NZ], zrecv.at[(z + k) % NZ], z_send.at[k - 1], z_recv.at[k - 1], at(dz=1)).wait_recv()

    def z_step(i, sums):
        at_rows = pl.ds(pl.multiple_of(i * 16, 16), 16)
        items = [zrecv[k, at_rows, :].astype(F32) for k in range(NZ)]
        out = []
        for s, (a, b) in zip(sums, ZPAIRS):
            product = items[a] * items[b]
            out.append(s + product[0:8] + product[8:16])
        return tuple(out)

    vec = to_lanes(lax.fori_loop(0, cols // 16, z_step, (zero,) * len(ZPAIRS)))
    vec = reduce_stage(vec, 2, zred, NZ, z, lambda k: at(dz=k))
    vec = reduce_stage(vec, 3, yred.at[1], NY, y, lambda k: at(dy=k))
    vec = reduce_stage(vec, 4, tred.at[1], NT, t, lambda k: at(dt=k))
    weights, first_sq, second_sq = tree(pick(vec, len(ZPAIRS)), ZPAIRS)
    total = weights[0] * zrecv[0].astype(F32)
    for k in range(1, NZ):
        total = total + weights[k] * zrecv[k].astype(F32)
    comb_out[...] = jnp.transpose(total)
    norm_out[...] = jnp.where(lane == 0, jnp.sqrt(first_sq), jnp.sqrt(second_sq)) * (1.0 / width)

    for k in (1, 2, 3):
        ref = gin.at[(y + k) % NY, my_rows]
        remote(ref, ref, iy_send.at[k - 1], iy_recv.at[k - 1], at(dy=k)).wait_send()
    for copy in e_copies + ix_copies + is_copies + p_copies + q_copies + z_copies:
        copy.wait_send()


def body(inputs, weight, targets, momentum):
    rows, width = inputs.shape
    cols = weight.shape[1]
    block = width // (NZ * NY)
    wide = block * NZ
    dma = pltpu.SemaphoreType.DMA
    any_spec = pl.BlockSpec(memory_space=pl.ANY)
    vmem = pl.BlockSpec(memory_space=pltpu.VMEM)
    summed, combined, norms = pl.pallas_call(
        kernel,
        out_shape=(
            jax.ShapeDtypeStruct((cols, rows), BF16),
            jax.ShapeDtypeStruct((block, cols), F32),
            jax.ShapeDtypeStruct((8, 128), F32),
        ),
        in_specs=[any_spec] * 3,
        out_specs=(vmem, vmem, vmem),
        scratch_shapes=[
            pltpu.VMEM((rows, width), BF16),
            pltpu.VMEM((width, cols), BF16),
            pltpu.VMEM((rows, cols), BF16),
            pltpu.VMEM((rows, cols), F32),
            pltpu.VMEM((NY, rows, wide), BF16),
            pltpu.VMEM((NY, cols, rows), BF16),
            pltpu.VMEM((NX, cols, rows), BF16),
            pltpu.VMEM((NX, cols, rows), BF16),
            pltpu.VMEM((NX, cols, rows), BF16),
            pltpu.VMEM((NX - 1, cols, rows), BF16),
            pltpu.VMEM((NY, cols, wide), F32),
            pltpu.VMEM((NZ - 1, cols, block), BF16),
            pltpu.VMEM((NZ, cols, block), BF16),
            pltpu.VMEM((128, 128), F32),
            pltpu.VMEM((2, NY, 8, 128), F32),
            pltpu.VMEM((2, NT, 8, 128), F32),
            pltpu.VMEM((NZ, 8, 128), F32),
            pltpu.VMEM((5, 8, 128), F32),
            dma((2 * KCHUNKS + 1,)),
            dma,
            dma((3,)), dma((3,)),
            dma((9,)), dma((9,)),
            dma((12,)), dma((12,)),
            dma((6,)), dma((6,)),
            dma((NX,)), dma((NX,)),
            dma((3,)), dma((3,)),
            dma((NZ - 1,)), dma((NZ - 1,)),
            dma((5,)), dma((5,)),
        ],
        compiler_params=pltpu.CompilerParams(
            collective_id=0, has_side_effects=True, vmem_limit_bytes=60 * 2**20
        ),
    )(inputs, weight, targets)
    return (summed, 0.9 * momentum + combined, norms[0, :2])


def solution(mesh):
    return jax.shard_map(
        body,
        mesh=mesh,
        in_specs=(P("dp", None), P(None, "tensor"), P("dp", "tensor"), P("dp", "tensor")),
        out_specs=(P("tensor", "dp"), P("dp", "tensor"), P()),
        check_vma=False,
    )
```

```python
import functools
import math

import jax
import jax.numpy as jnp
from jax import lax
from jax.experimental import pallas as pl
from jax.experimental.pallas import tpu as pltpu
from jax.sharding import PartitionSpec as P

MESH = pl.DeviceIdType.MESH
NZ, NY, NX, NC = 8, 4, 4, 2
NT = NX * NC
F32, BF16 = jnp.float32, jnp.bfloat16
KCHUNKS = 4
YPAIRS = [(i, j) for i in range(NY) for j in range(i, NY)]
ZPAIRS = [(i, j) for i in range(NZ) for j in range(i, NZ)]


def tree(gram, pairs):
    count = max(j for _, j in pairs) + 1
    value = {}
    for at, (i, j) in enumerate(pairs):
        value[i, j] = value[j, i] = gram[at]
    items = [{i: None} for i in range(count)]

    def weighted(term, coefficient):
        return term if coefficient is None else term * coefficient

    def inner(first, second):
        total = None
        for i, a in first.items():
            for j, c in second.items():
                term = weighted(weighted(value[i, j], a), c)
                total = term if total is None else total + term
        return total

    while len(items) > 1:
        merged = []
        for at in range(0, len(items), 2):
            first, second = items[at], items[at + 1]
            cross, first_sq, second_sq = inner(first, second), inner(first, first), inner(second, second)
            left = 1.0 - cross / (2.0 * first_sq)
            right = 1.0 - cross / (2.0 * second_sq)
            item = {i: weighted(left, a) for i, a in first.items()}
            item.update({i: weighted(right, c) for i, c in second.items()})
            merged.append(item)
        items = merged
    return [items[0][i] for i in range(count)], first_sq, second_sq


def kernel(
    inputs, weight, targets,
    ig_out, comb_out, norm_out,
    ig, comb, norm, gacc,
    xin, w, tg, acc, gin, et, psend, precv, ppart, xrecv, gbuf, zsend, zrecv,
    gsum, yred, tred, zred, mine,
    ld_sem, out_sem, own_sem, iy_send, iy_recv, ix_send, ix_recv, is_send, is_recv,
    e_send, e_recv, p_send, p_recv, q_send, q_recv, z_send, z_recv, r_send, r_recv,
):
    dp, t = lax.axis_index("dp"), lax.axis_index("tensor")
    z, y, x, c = dp // NY, dp % NY, t // NC, t % NC
    rows, width = inputs.shape
    cols = weight.shape[1]
    kc = width // KCHUNKS
    part_rows = rows // NT
    block = width // (NZ * NY)
    wide = block * NZ

    def at(dz=0, dy=0, dt=None):
        return ((z + dz) % NZ * NY + (y + dy) % NY, t if dt is None else (t + dt) % NT)

    def at_x(dx, core):
        return (dp, (x + dx) % NX * NC + core)

    loads = []
    for i in range(KCHUNKS):
        a = pltpu.make_async_copy(inputs.at[:, i * kc:(i + 1) * kc], xin.at[:, i * kc:(i + 1) * kc], ld_sem.at[2 * i])
        b = pltpu.make_async_copy(weight.at[i * kc:(i + 1) * kc], w.at[i * kc:(i + 1) * kc], ld_sem.at[2 * i + 1])
        a.start()
        b.start()
        loads.append((a, b))
    tg_load = pltpu.make_async_copy(targets, tg, ld_sem.at[2 * KCHUNKS])
    tg_load.start()

    barrier = pltpu.get_barrier_semaphore()
    peers = [at(dz=k) for k in range(1, NZ)] + [at(dy=k) for k in range(1, NY)] + [at(dt=k) for k in range(1, NT)]
    for peer in peers:
        pl.semaphore_signal(barrier, inc=1, device_id=peer, device_id_type=MESH)
    pl.semaphore_wait(barrier, len(peers))

    def remote(src, dst, send, recv, peer):
        return pltpu.make_async_remote_copy(
            src_ref=src, dst_ref=dst, send_sem=send, recv_sem=recv, device_id=peer, device_id_type=MESH
        )

    my_rows = pl.ds(pl.multiple_of(t * part_rows, part_rows), part_rows)
    for k in (1, 3, 2):
        for b in range(NZ):
            col = pl.multiple_of((b * NY + (y + k) % NY) * block, block)
            remote(
                inputs.at[my_rows, pl.ds(col, block)], gin.at[y, my_rows, b * block:(b + 1) * block],
                iy_send.at[k - 1], iy_recv.at[3 - k], at(dy=k),
            ).start()
    for b in range(NZ):
        col = pl.multiple_of((b * NY + y) * block, block)
        pltpu.make_async_copy(inputs.at[:, pl.ds(col, block)], gin.at[y, :, b * block:(b + 1) * block], own_sem).start()

    for i, (a, b) in enumerate(loads):
        a.wait()
        b.wait()
        part = jnp.dot(xin[:, i * kc:(i + 1) * kc], w[i * kc:(i + 1) * kc, :], preferred_element_type=F32)
        if i == 0:
            acc[...] = part
        else:
            acc[...] += part
    tg_load.wait()
    et[y] = jnp.transpose((acc[...] - tg[...].astype(F32)).astype(BF16))

    half = cols // 2
    low, high = pl.ds(0, half), pl.ds(half, half)
    right, left, across = (y + 1) % NY, (y + 3) % NY, (y + 2) % NY

    def send_error(index, sem, part, dy):
        copy = remote(et.at[index, part], et.at[index, part], e_send.at[sem], e_recv.at[sem], at(dy=dy))
        copy.start()
        return copy

    e_copies = [
        send_error(y, 0, low, 3),
        send_error(y, 3, high, 1),
        send_error(y, 1, high, 3),
        send_error(y, 2, low, 1),
    ]

    def e_wait(index, sem, part):
        remote(et.at[index, part], et.at[index, part], e_send.at[sem], e_recv.at[sem], at(dy=1)).wait_recv()

    sib = at_x(0, 1 - c)
    def rows_of(dx, core):
        return pl.multiple_of(((x + dx) % NX * NC + core) * part_rows, part_rows)

    sub = part_rows // 2
    copies = []

    def share(k, start, count, sends, recvs, sem, peer):
        ref = gin.at[(y + k) % NY, pl.ds(start, count)]
        copy = remote(ref, ref, sends.at[sem], recvs.at[sem], peer)
        copy.start()
        copies.append(copy)

    def shared(k, start, count, sends, recvs, sem):
        ref = gin.at[(y + k) % NY, pl.ds(start, count)]
        remote(ref, ref, sends.at[sem], recvs.at[sem], sib).wait_recv()

    mine_low = rows_of(0, c)
    mine_high = mine_low + sub
    right_low = rows_of(1, c)
    left_low = rows_of(3, c)
    across_low = rows_of(2, c)
    order = (1, 3, 2)
    for k in order:
        ref = gin.at[(y + k) % NY, my_rows]
        remote(ref, ref, iy_send.at[k - 1], iy_recv.at[k - 1], at(dy=k)).wait_recv()
        share(k, mine_low, sub, ix_send, ix_recv, k - 1, at_x(3, c))
        share(k, mine_high, sub, ix_send, ix_recv, 6 + k - 1, at_x(1, c))
        share(k, mine_high, sub, ix_send, ix_recv, 3 + k - 1, at_x(3, c))
        share(k, mine_low, sub, ix_send, ix_recv, 9 + k - 1, at_x(1, c))
        share(k, mine_low, part_rows, is_send, is_recv, k - 1, sib)

    p_copies = []
    for j in range(NX):
        start = pl.multiple_of(((x + j) % NX * NC + 1 - c) * cols, cols)
        psend[j] = jnp.dot(w[pl.ds(start, cols), :], et[y], preferred_element_type=F32).astype(BF16)
        copy = remote(psend.at[j], precv.at[j], p_send.at[j], p_recv.at[j], sib)
        copy.start()
        p_copies.append(copy)
    for j in range(NX):
        start = pl.multiple_of(((x + j) % NX * NC + c) * cols, cols)
        ppart[j] = jnp.dot(w[pl.ds(start, cols), :], et[y], preferred_element_type=F32).astype(BF16)

    def gradient(index):
        gbuf[index] = jnp.dot(et[index], gin[index], preferred_element_type=F32)

    pltpu.make_async_copy(gin.at[y], gin.at[y], own_sem).wait()
    gradient(y)

    for k in order:
        shared(k, right_low, sub, ix_send, ix_recv, k - 1)
        share(k, right_low, sub, ix_send, ix_recv, 12 + k - 1, at_x(3, c))
        shared(k, left_low + sub, sub, ix_send, ix_recv, 6 + k - 1)
        share(k, left_low + sub, sub, ix_send, ix_recv, 15 + k - 1, at_x(1, c))
    e_wait(right, 0, low)
    e_copies.append(send_error(right, 4, low, 3))
    e_wait(left, 3, high)
    e_copies.append(send_error(left, 5, high, 1))
    for j in range(NX):
        p_copies[j].wait_recv()
        ppart[j] = (ppart[j].astype(F32) + precv[j].astype(F32)).astype(BF16)
    for k in order:
        shared(k, right_low + sub, sub, ix_send, ix_recv, 3 + k - 1)
        share(k, right_low, part_rows, is_send, is_recv, 3 + k - 1, sib)
        shared(k, left_low, sub, ix_send, ix_recv, 9 + k - 1)
        share(k, left_low, part_rows, is_send, is_recv, 6 + k - 1, sib)
    for k in order:
        shared(k, across_low, sub, ix_send, ix_recv, 12 + k - 1)
        shared(k, across_low + sub, sub, ix_send, ix_recv, 15 + k - 1)
        share(k, across_low, part_rows, is_send, is_recv, 9 + k - 1, sib)

    def inputs_wait(k):
        for n, dx in enumerate((0, 1, 3, 2)):
            shared(k, rows_of(dx, 1 - c), part_rows, is_send, is_recv, 3 * n + k - 1)

    def fold(value):
        total = value[:, 0:128]
        for l in range(1, value.shape[1] // 128):
            total = total + value[:, l * 128:(l + 1) * 128]
        return total

    zero = jnp.zeros((8, 128), F32)

    def inner_products(items, pairs):
        def step(i, sums):
            at_rows = pl.ds(pl.multiple_of(i * 8, 8), 8)
            values = [gbuf[k, at_rows, :] for k in items]
            return tuple(s + fold(values[a] * values[b]) for s, (a, b) in zip(sums, pairs))

        sums = lax.fori_loop(0, cols // 8, step, (zero,) * len(pairs))
        for value, (a, b) in zip(sums, pairs):
            low_index, high_index = jnp.minimum(items[a], items[b]), jnp.maximum(items[a], items[b])
            gacc[low_index * NY + high_index] = value

    e_wait(right, 1, high)
    inputs_wait(1)
    gradient(right)
    e_wait(left, 2, low)
    inputs_wait(3)
    gradient(left)
    inner_products([y, right, left], [(0, 0), (0, 1), (0, 2), (1, 1), (1, 2), (2, 2)])
    inputs_wait(2)
    e_wait(across, 4, low)
    e_wait(across, 5, high)
    gradient(across)
    inner_products([across, y, right, left], [(0, 0), (0, 1), (0, 2), (0, 3)])

    gsum[...] = jnp.zeros_like(gsum)
    ones = jnp.ones((8, 128), F32)
    lane = lax.broadcasted_iota(jnp.int32, (8, 128), 1)

    def to_lanes(sums):
        for p, value in enumerate(sums):
            gsum[p:p + 1, :] = jnp.sum(value, axis=0, keepdims=True)
        return lax.dot_general(
            ones, gsum[...], (((1,), (1,)), ((), ())), precision=lax.Precision.HIGHEST, preferred_element_type=F32
        )

    def reduce_stage(value, slot, buffer, count, me, peer_of):
        mine[slot] = value
        buffer[me] = value
        for k in range(1, count):
            remote(mine.at[slot], buffer.at[me], r_send.at[slot], r_recv.at[slot], peer_of(k)).start()
        some = buffer.at[0:count - 1]
        remote(some, some, r_send.at[slot], r_recv.at[slot], peer_of(1)).wait()
        total = buffer[0]
        for k in range(1, count):
            total = total + buffer[k]
        return total

    def pick(vec, count):
        return [
            jnp.sum(jnp.where(lane == p, vec, 0.0), axis=1, keepdims=True)[0:1, :] for p in range(count)
        ]

    vec = to_lanes([gacc[a * NY + b] for a, b in YPAIRS])
    vec = reduce_stage(vec, 0, yred.at[0], NY, y, lambda k: at(dy=k))
    vec = reduce_stage(vec, 1, tred.at[0], NT, t, lambda k: at(dt=k))
    weights, _, _ = tree(pick(vec, len(YPAIRS)), YPAIRS)
    weights = [v * (1.0 / math.sqrt(rows)) for v in weights]

    def combine(b):
        lanes = pl.ds(pl.multiple_of(b * block, block), block)
        total = weights[0] * gbuf[0, :, lanes]
        for k in range(1, NY):
            total = total + weights[k] * gbuf[k, :, lanes]
        return total.astype(BF16)

    z_copies = []
    for k in (4, 3, 5, 2, 6, 1, 7):
        b = (z + k) % NZ
        zsend[k - 1] = combine(b)
        copy = remote(zsend.at[k - 1], zrecv.at[z], z_send.at[k - 1], z_recv.at[NZ - 1 - k], at(dz=k))
        copy.start()
        z_copies.append(copy)
    zrecv[z] = combine(z)

    q_copies = []
    for j in (2, 1, 3):
        copy = remote(ppart.at[j], xrecv.at[3 - j], q_send.at[j - 1], q_recv.at[3 - j], at_x(j, c))
        copy.start()
        q_copies.append(copy)
    for k in (1, 2, 3):
        ref = gin.at[(y + k) % NY, my_rows]
        remote(ref, ref, iy_send.at[k - 1], iy_recv.at[k - 1], at(dy=k)).wait_send()
    for copy in e_copies + copies + p_copies:
        copy.wait_send()
    for copy in q_copies:
        copy.wait_recv()
    total = ppart[0].astype(F32)
    for j in range(NX - 1):
        total = total + xrecv[j].astype(F32)
    ig[...] = total.astype(BF16)
    ig_copy = pltpu.make_async_copy(ig, ig_out, out_sem.at[0])
    ig_copy.start()
    for copy in q_copies:
        copy.wait_send()

    for k in range(1, NZ):
        remote(zrecv.at[(z + k) % NZ], zrecv.at[(z + k) % NZ], z_send.at[k - 1], z_recv.at[k - 1], at(dz=1)).wait_recv()

    def z_step(i, sums):
        at_rows = pl.ds(pl.multiple_of(i * 16, 16), 16)
        items = [zrecv[k, at_rows, :].astype(F32) for k in range(NZ)]
        out = []
        for s, (a, b) in zip(sums, ZPAIRS):
            product = items[a] * items[b]
            out.append(s + product[0:8] + product[8:16])
        return tuple(out)

    vec = to_lanes(lax.fori_loop(0, cols // 16, z_step, (zero,) * len(ZPAIRS)))
    vec = reduce_stage(vec, 2, zred, NZ, z, lambda k: at(dz=k))
    vec = reduce_stage(vec, 3, yred.at[1], NY, y, lambda k: at(dy=k))
    vec = reduce_stage(vec, 4, tred.at[1], NT, t, lambda k: at(dt=k))
    weights, first_sq, second_sq = tree(pick(vec, len(ZPAIRS)), ZPAIRS)
    total = weights[0] * zrecv[0].astype(F32)
    for k in range(1, NZ):
        total = total + weights[k] * zrecv[k].astype(F32)
    comb[...] = jnp.transpose(total)
    comb_copy = pltpu.make_async_copy(comb, comb_out, out_sem.at[1])
    comb_copy.start()
    norm[...] = jnp.where(lane == 0, jnp.sqrt(first_sq), jnp.sqrt(second_sq)) * (1.0 / width)
    norm_copy = pltpu.make_async_copy(norm, norm_out, out_sem.at[2])
    norm_copy.start()
    for copy in z_copies:
        copy.wait_send()
    ig_copy.wait()
    comb_copy.wait()
    norm_copy.wait()


def finish(ig, comb, norm, momentum, ig_out, momentum_out, norm_out):
    ig_out[...] = ig[...]
    momentum_out[...] = 0.9 * momentum[...] + comb[...]
    norm_out[0] = norm[0, 0]
    norm_out[1] = norm[0, 1]


def body(inputs, weight, targets, momentum):
    rows, width = inputs.shape
    cols = weight.shape[1]
    block = width // (NZ * NY)
    wide = block * NZ
    dma = pltpu.SemaphoreType.DMA
    any_spec = pl.BlockSpec(memory_space=pl.ANY)
    vmem = pl.BlockSpec(memory_space=pltpu.VMEM)
    summed, combined, norms = pl.pallas_call(
        kernel,
        out_shape=(
            jax.ShapeDtypeStruct((cols, rows), BF16),
            jax.ShapeDtypeStruct((block, cols), F32),
            jax.ShapeDtypeStruct((8, 128), F32),
        ),
        in_specs=[any_spec] * 3,
        out_specs=(any_spec,) * 3,
        scratch_shapes=[
            pltpu.VMEM((cols, rows), BF16),
            pltpu.VMEM((block, cols), F32),
            pltpu.VMEM((8, 128), F32),
            pltpu.VMEM((NY * NY, 8, 128), F32),
            pltpu.VMEM((rows, width), BF16),
            pltpu.VMEM((width, cols), BF16),
            pltpu.VMEM((rows, cols), BF16),
            pltpu.VMEM((rows, cols), F32),
            pltpu.VMEM((NY, rows, wide), BF16),
            pltpu.VMEM((NY, cols, rows), BF16),
            pltpu.VMEM((NX, cols, rows), BF16),
            pltpu.VMEM((NX, cols, rows), BF16),
            pltpu.VMEM((NX, cols, rows), BF16),
            pltpu.VMEM((NX - 1, cols, rows), BF16),
            pltpu.VMEM((NY, cols, wide), F32),
            pltpu.VMEM((NZ - 1, cols, block), BF16),
            pltpu.VMEM((NZ, cols, block), BF16),
            pltpu.VMEM((128, 128), F32),
            pltpu.VMEM((2, NY, 8, 128), F32),
            pltpu.VMEM((2, NT, 8, 128), F32),
            pltpu.VMEM((NZ, 8, 128), F32),
            pltpu.VMEM((5, 8, 128), F32),
            dma((2 * KCHUNKS + 1,)),
            dma((3,)),
            dma,
            dma((3,)), dma((3,)),
            dma((18,)), dma((18,)),
            dma((12,)), dma((12,)),
            dma((6,)), dma((6,)),
            dma((NX,)), dma((NX,)),
            dma((3,)), dma((3,)),
            dma((NZ - 1,)), dma((NZ - 1,)),
            dma((5,)), dma((5,)),
        ],
        compiler_params=pltpu.CompilerParams(
            collective_id=0, has_side_effects=True, vmem_limit_bytes=60 * 2**20
        ),
    )(inputs, weight, targets)
    smem = pl.BlockSpec(memory_space=pltpu.SMEM)
    return pl.pallas_call(
        finish,
        out_shape=(
            jax.ShapeDtypeStruct((cols, rows), BF16),
            jax.ShapeDtypeStruct((block, cols), F32),
            jax.ShapeDtypeStruct((2,), F32),
        ),
        in_specs=[vmem, vmem, smem, vmem],
        out_specs=(vmem, vmem, smem),
    )(summed, combined, norms, momentum)


def solution(mesh):
    return jax.shard_map(
        body,
        mesh=mesh,
        in_specs=(P("dp", None), P(None, "tensor"), P("dp", "tensor"), P("dp", "tensor")),
        out_specs=(P("tensor", "dp"), P("dp", "tensor"), P()),
        check_vma=False,
    )
```

```python
import functools
import math

import jax
import jax.numpy as jnp
from jax import lax
from jax.experimental import pallas as pl
from jax.experimental.pallas import tpu as pltpu
from jax.sharding import PartitionSpec as P

MESH = pl.DeviceIdType.MESH
NZ, NY, NX, NC = 8, 4, 4, 2
NT = NX * NC
F32, BF16 = jnp.float32, jnp.bfloat16
KCHUNKS = 4
YPAIRS = [(i, j) for i in range(NY) for j in range(i, NY)]
ZPAIRS = [(i, j) for i in range(NZ) for j in range(i, NZ)]


def tree(gram, pairs):
    count = max(j for _, j in pairs) + 1
    value = {}
    for at, (i, j) in enumerate(pairs):
        value[i, j] = value[j, i] = gram[at]
    items = [{i: None} for i in range(count)]

    def weighted(term, coefficient):
        return term if coefficient is None else term * coefficient

    def inner(first, second):
        total = None
        for i, a in first.items():
            for j, c in second.items():
                term = weighted(weighted(value[i, j], a), c)
                total = term if total is None else total + term
        return total

    while len(items) > 1:
        merged = []
        for at in range(0, len(items), 2):
            first, second = items[at], items[at + 1]
            cross, first_sq, second_sq = inner(first, second), inner(first, first), inner(second, second)
            left = 1.0 - cross / (2.0 * first_sq)
            right = 1.0 - cross / (2.0 * second_sq)
            item = {i: weighted(left, a) for i, a in first.items()}
            item.update({i: weighted(right, c) for i, c in second.items()})
            merged.append(item)
        items = merged
    return [items[0][i] for i in range(count)], first_sq, second_sq


def kernel(
    inputs, weight, targets,
    ig_out, comb_out, norm_out,
    ig, comb, norm, gacc,
    xin, w, tg, acc, gin, et, psend, precv, ppart, xrecv, gbuf, zsend, zrecv,
    gsum, red, zred, mine,
    ld_sem, out_sem, own_sem, iy_send, iy_recv, ix_send, ix_recv, is_send, is_recv,
    e_send, e_recv, p_send, p_recv, q_send, q_recv, z_send, z_recv, r_send, r_recv,
):
    dp, t = lax.axis_index("dp"), lax.axis_index("tensor")
    z, y, x, c = dp // NY, dp % NY, t // NC, t % NC
    rows, width = inputs.shape
    cols = weight.shape[1]
    kc = width // KCHUNKS
    part_rows = rows // NT
    block = width // (NZ * NY)
    wide = block * NZ

    def at(dz=0, dy=0, dt=None):
        return ((z + dz) % NZ * NY + (y + dy) % NY, t if dt is None else (t + dt) % NT)

    def at_x(dx, core):
        return (dp, (x + dx) % NX * NC + core)

    loads = []
    for i in range(KCHUNKS):
        a = pltpu.make_async_copy(inputs.at[:, i * kc:(i + 1) * kc], xin.at[:, i * kc:(i + 1) * kc], ld_sem.at[2 * i])
        b = pltpu.make_async_copy(weight.at[i * kc:(i + 1) * kc], w.at[i * kc:(i + 1) * kc], ld_sem.at[2 * i + 1])
        a.start()
        b.start()
        loads.append((a, b))
    tg_load = pltpu.make_async_copy(targets, tg, ld_sem.at[2 * KCHUNKS])
    tg_load.start()

    barrier = pltpu.get_barrier_semaphore()
    line = [at(dz=k) for k in (4, 3, 5, 2, 6, 1, 7)]
    plane = [
        (z * NY + (y + dy) % NY, (x + dx) % NX * NC + (c + dc) % NC)
        for dx in (2, 1, 3, 0) for dy in (2, 1, 3, 0) for dc in range(NC) if dx or dy or dc
    ]
    peers = line + plane
    for peer in peers:
        pl.semaphore_signal(barrier, inc=1, device_id=peer, device_id_type=MESH)
    pl.semaphore_wait(barrier, len(peers))

    def remote(src, dst, send, recv, peer):
        return pltpu.make_async_remote_copy(
            src_ref=src, dst_ref=dst, send_sem=send, recv_sem=recv, device_id=peer, device_id_type=MESH
        )

    my_rows = pl.ds(pl.multiple_of(t * part_rows, part_rows), part_rows)
    for k in (1, 3, 2):
        for b in range(NZ):
            col = pl.multiple_of((b * NY + (y + k) % NY) * block, block)
            remote(
                inputs.at[my_rows, pl.ds(col, block)], gin.at[y, my_rows, b * block:(b + 1) * block],
                iy_send.at[k - 1], iy_recv.at[3 - k], at(dy=k),
            ).start()
    for b in range(NZ):
        col = pl.multiple_of((b * NY + y) * block, block)
        pltpu.make_async_copy(inputs.at[:, pl.ds(col, block)], gin.at[y, :, b * block:(b + 1) * block], own_sem).start()

    for i, (a, b) in enumerate(loads):
        a.wait()
        b.wait()
        part = jnp.dot(xin[:, i * kc:(i + 1) * kc], w[i * kc:(i + 1) * kc, :], preferred_element_type=F32)
        if i == 0:
            acc[...] = part
        else:
            acc[...] += part
    tg_load.wait()
    et[y] = jnp.transpose((acc[...] - tg[...].astype(F32)).astype(BF16))

    half = cols // 2
    low, high = pl.ds(0, half), pl.ds(half, half)
    right, left, across = (y + 1) % NY, (y + 3) % NY, (y + 2) % NY

    def send_error(index, sem, part, dy):
        copy = remote(et.at[index, part], et.at[index, part], e_send.at[sem], e_recv.at[sem], at(dy=dy))
        copy.start()
        return copy

    e_copies = [
        send_error(y, 0, low, 3),
        send_error(y, 3, high, 1),
        send_error(y, 1, high, 3),
        send_error(y, 2, low, 1),
    ]

    def e_wait(index, sem, part):
        remote(et.at[index, part], et.at[index, part], e_send.at[sem], e_recv.at[sem], at(dy=1)).wait_recv()

    sib = at_x(0, 1 - c)
    def rows_of(dx, core):
        return pl.multiple_of(((x + dx) % NX * NC + core) * part_rows, part_rows)

    sub = part_rows // 2
    copies = []

    def share(k, start, count, sends, recvs, sem, peer):
        ref = gin.at[(y + k) % NY, pl.ds(start, count)]
        copy = remote(ref, ref, sends.at[sem], recvs.at[sem], peer)
        copy.start()
        copies.append(copy)

    def shared(k, start, count, sends, recvs, sem):
        ref = gin.at[(y + k) % NY, pl.ds(start, count)]
        remote(ref, ref, sends.at[sem], recvs.at[sem], sib).wait_recv()

    mine_low = rows_of(0, c)
    mine_high = mine_low + sub
    right_low = rows_of(1, c)
    left_low = rows_of(3, c)
    across_low = rows_of(2, c)
    order = (1, 3, 2)
    for k in order:
        ref = gin.at[(y + k) % NY, my_rows]
        remote(ref, ref, iy_send.at[k - 1], iy_recv.at[k - 1], at(dy=k)).wait_recv()
        share(k, mine_low, sub, ix_send, ix_recv, k - 1, at_x(3, c))
        share(k, mine_high, sub, ix_send, ix_recv, 6 + k - 1, at_x(1, c))
        share(k, mine_high, sub, ix_send, ix_recv, 3 + k - 1, at_x(3, c))
        share(k, mine_low, sub, ix_send, ix_recv, 9 + k - 1, at_x(1, c))
        share(k, mine_low, part_rows, is_send, is_recv, k - 1, sib)

    p_copies = []
    for j in range(NX):
        start = pl.multiple_of(((x + j) % NX * NC + 1 - c) * cols, cols)
        psend[j] = jnp.dot(w[pl.ds(start, cols), :], et[y], preferred_element_type=F32).astype(BF16)
        copy = remote(psend.at[j], precv.at[j], p_send.at[j], p_recv.at[j], sib)
        copy.start()
        p_copies.append(copy)
    for j in range(NX):
        start = pl.multiple_of(((x + j) % NX * NC + c) * cols, cols)
        ppart[j] = jnp.dot(w[pl.ds(start, cols), :], et[y], preferred_element_type=F32).astype(BF16)

    def gradient(index):
        gbuf[index] = jnp.dot(et[index], gin[index], preferred_element_type=F32)

    pltpu.make_async_copy(gin.at[y], gin.at[y], own_sem).wait()
    gradient(y)

    for k in order:
        shared(k, right_low, sub, ix_send, ix_recv, k - 1)
        share(k, right_low, sub, ix_send, ix_recv, 12 + k - 1, at_x(3, c))
        shared(k, left_low + sub, sub, ix_send, ix_recv, 6 + k - 1)
        share(k, left_low + sub, sub, ix_send, ix_recv, 15 + k - 1, at_x(1, c))
    e_wait(right, 0, low)
    e_copies.append(send_error(right, 4, low, 3))
    e_wait(left, 3, high)
    e_copies.append(send_error(left, 5, high, 1))
    for j in range(NX):
        p_copies[j].wait_recv()
        ppart[j] = (ppart[j].astype(F32) + precv[j].astype(F32)).astype(BF16)
    for k in order:
        shared(k, right_low + sub, sub, ix_send, ix_recv, 3 + k - 1)
        share(k, right_low, part_rows, is_send, is_recv, 3 + k - 1, sib)
        shared(k, left_low, sub, ix_send, ix_recv, 9 + k - 1)
        share(k, left_low, part_rows, is_send, is_recv, 6 + k - 1, sib)
    for k in order:
        shared(k, across_low, sub, ix_send, ix_recv, 12 + k - 1)
        shared(k, across_low + sub, sub, ix_send, ix_recv, 15 + k - 1)
        share(k, across_low, part_rows, is_send, is_recv, 9 + k - 1, sib)

    def inputs_wait(k):
        for n, dx in enumerate((0, 1, 3, 2)):
            shared(k, rows_of(dx, 1 - c), part_rows, is_send, is_recv, 3 * n + k - 1)

    def fold(value):
        total = value[:, 0:128]
        for l in range(1, value.shape[1] // 128):
            total = total + value[:, l * 128:(l + 1) * 128]
        return total

    zero = jnp.zeros((8, 128), F32)

    def inner_products(items, pairs):
        def step(i, sums):
            at_rows = pl.ds(pl.multiple_of(i * 8, 8), 8)
            values = [gbuf[k, at_rows, :] for k in items]
            return tuple(s + fold(values[a] * values[b]) for s, (a, b) in zip(sums, pairs))

        sums = lax.fori_loop(0, cols // 8, step, (zero,) * len(pairs))
        for value, (a, b) in zip(sums, pairs):
            low_index, high_index = jnp.minimum(items[a], items[b]), jnp.maximum(items[a], items[b])
            gacc[low_index * NY + high_index] = value

    e_wait(right, 1, high)
    inputs_wait(1)
    gradient(right)
    e_wait(left, 2, low)
    inputs_wait(3)
    gradient(left)
    inner_products([y, right, left], [(0, 0), (0, 1), (0, 2), (1, 1), (1, 2), (2, 2)])
    inputs_wait(2)
    e_wait(across, 4, low)
    e_wait(across, 5, high)
    gradient(across)
    inner_products([across, y, right, left], [(0, 0), (0, 1), (0, 2), (0, 3)])

    gsum[...] = jnp.zeros_like(gsum)
    ones = jnp.ones((8, 128), F32)
    lane = lax.broadcasted_iota(jnp.int32, (8, 128), 1)

    def to_lanes(sums):
        for p, value in enumerate(sums):
            gsum[p:p + 1, :] = jnp.sum(value, axis=0, keepdims=True)
        return lax.dot_general(
            ones, gsum[...], (((1,), (1,)), ((), ())), precision=lax.Precision.HIGHEST, preferred_element_type=F32
        )[0:1, :]

    def reduce_stage(value, slot, buffer, me, peers_of):
        mine[slot] = value
        buffer[me] = value
        for peer in peers_of:
            remote(mine.at[slot], buffer.at[me], r_send.at[slot], r_recv.at[slot], peer).start()
        count = len(peers_of)
        some = buffer.at[0:count]
        remote(some, some, r_send.at[slot], r_recv.at[slot], peers_of[0]).wait()
        total = buffer[0]
        for k in range(1, count + 1):
            total = total + buffer[k]
        return total

    def pick(vec, count):
        return [
            jnp.sum(jnp.where(lane[0:1] == p, vec, 0.0), axis=1, keepdims=True) for p in range(count)
        ]

    vec = to_lanes([gacc[a * NY + b] for a, b in YPAIRS])
    vec = reduce_stage(vec, 0, red.at[0], y * NT + t, plane)
    weights, _, _ = tree(pick(vec, len(YPAIRS)), YPAIRS)
    weights = [v * (1.0 / math.sqrt(rows)) for v in weights]

    def combine(b):
        lanes = pl.ds(pl.multiple_of(b * block, block), block)
        total = weights[0] * gbuf[0, :, lanes]
        for k in range(1, NY):
            total = total + weights[k] * gbuf[k, :, lanes]
        return total.astype(BF16)

    z_copies = []
    for k in (4, 3, 5, 2, 6, 1, 7):
        b = (z + k) % NZ
        zsend[k - 1] = combine(b)
        copy = remote(zsend.at[k - 1], zrecv.at[z], z_send.at[k - 1], z_recv.at[NZ - 1 - k], at(dz=k))
        copy.start()
        z_copies.append(copy)
    zrecv[z] = combine(z)

    q_copies = []
    for j in (2, 1, 3):
        copy = remote(ppart.at[j], xrecv.at[3 - j], q_send.at[j - 1], q_recv.at[3 - j], at_x(j, c))
        copy.start()
        q_copies.append(copy)
    for k in (1, 2, 3):
        ref = gin.at[(y + k) % NY, my_rows]
        remote(ref, ref, iy_send.at[k - 1], iy_recv.at[k - 1], at(dy=k)).wait_send()
    for copy in e_copies + copies + p_copies:
        copy.wait_send()
    for copy in q_copies:
        copy.wait_recv()
    total = ppart[0].astype(F32)
    for j in range(NX - 1):
        total = total + xrecv[j].astype(F32)
    ig[...] = total.astype(BF16)
    ig_copy = pltpu.make_async_copy(ig, ig_out, out_sem.at[0])
    ig_copy.start()
    for copy in q_copies:
        copy.wait_send()

    for k in range(1, NZ):
        remote(zrecv.at[(z + k) % NZ], zrecv.at[(z + k) % NZ], z_send.at[k - 1], z_recv.at[k - 1], at(dz=1)).wait_recv()

    def z_step(i, sums):
        at_rows = pl.ds(pl.multiple_of(i * 16, 16), 16)
        items = [zrecv[k, at_rows, :].astype(F32) for k in range(NZ)]
        out = []
        for s, (a, b) in zip(sums, ZPAIRS):
            product = items[a] * items[b]
            out.append(s + product[0:8] + product[8:16])
        return tuple(out)

    vec = to_lanes(lax.fori_loop(0, cols // 16, z_step, (zero,) * len(ZPAIRS)))
    vec = reduce_stage(vec, 1, zred, z, line)
    vec = reduce_stage(vec, 2, red.at[1], y * NT + t, plane)
    weights, first_sq, second_sq = tree(pick(vec, len(ZPAIRS)), ZPAIRS)
    total = weights[0] * zrecv[0].astype(F32)
    for k in range(1, NZ):
        total = total + weights[k] * zrecv[k].astype(F32)
    comb[...] = jnp.transpose(total)
    comb_copy = pltpu.make_async_copy(comb, comb_out, out_sem.at[1])
    comb_copy.start()
    norm[...] = jnp.where(lane[0:1] == 0, jnp.sqrt(first_sq), jnp.sqrt(second_sq)) * (1.0 / width)
    norm_copy = pltpu.make_async_copy(norm, norm_out, out_sem.at[2])
    norm_copy.start()
    for copy in z_copies:
        copy.wait_send()
    ig_copy.wait()
    comb_copy.wait()
    norm_copy.wait()


def finish(ig, comb, norm, momentum, ig_out, momentum_out, norm_out):
    ig_out[...] = ig[...]
    momentum_out[...] = 0.9 * momentum[...] + comb[...]
    norm_out[0] = norm[0, 0]
    norm_out[1] = norm[0, 1]


def body(inputs, weight, targets, momentum):
    rows, width = inputs.shape
    cols = weight.shape[1]
    block = width // (NZ * NY)
    wide = block * NZ
    dma = pltpu.SemaphoreType.DMA
    any_spec = pl.BlockSpec(memory_space=pl.ANY)
    vmem = pl.BlockSpec(memory_space=pltpu.VMEM)
    summed, combined, norms = pl.pallas_call(
        kernel,
        out_shape=(
            jax.ShapeDtypeStruct((cols, rows), BF16),
            jax.ShapeDtypeStruct((block, cols), F32),
            jax.ShapeDtypeStruct((1, 128), F32),
        ),
        in_specs=[any_spec] * 3,
        out_specs=(any_spec,) * 3,
        scratch_shapes=[
            pltpu.VMEM((cols, rows), BF16),
            pltpu.VMEM((block, cols), F32),
            pltpu.VMEM((1, 128), F32),
            pltpu.VMEM((NY * NY, 8, 128), F32),
            pltpu.VMEM((rows, width), BF16),
            pltpu.VMEM((width, cols), BF16),
            pltpu.VMEM((rows, cols), BF16),
            pltpu.VMEM((rows, cols), F32),
            pltpu.VMEM((NY, rows, wide), BF16),
            pltpu.VMEM((NY, cols, rows), BF16),
            pltpu.VMEM((NX, cols, rows), BF16),
            pltpu.VMEM((NX, cols, rows), BF16),
            pltpu.VMEM((NX, cols, rows), BF16),
            pltpu.VMEM((NX - 1, cols, rows), BF16),
            pltpu.VMEM((NY, cols, wide), F32),
            pltpu.VMEM((NZ - 1, cols, block), BF16),
            pltpu.VMEM((NZ, cols, block), BF16),
            pltpu.VMEM((128, 128), F32),
            pltpu.VMEM((2, NY * NT, 1, 128), F32),
            pltpu.VMEM((NZ, 1, 128), F32),
            pltpu.VMEM((3, 1, 128), F32),
            dma((2 * KCHUNKS + 1,)),
            dma((3,)),
            dma,
            dma((3,)), dma((3,)),
            dma((18,)), dma((18,)),
            dma((12,)), dma((12,)),
            dma((6,)), dma((6,)),
            dma((NX,)), dma((NX,)),
            dma((3,)), dma((3,)),
            dma((NZ - 1,)), dma((NZ - 1,)),
            dma((3,)), dma((3,)),
        ],
        compiler_params=pltpu.CompilerParams(
            collective_id=0, has_side_effects=True, vmem_limit_bytes=60 * 2**20
        ),
    )(inputs, weight, targets)
    smem = pl.BlockSpec(memory_space=pltpu.SMEM)
    return pl.pallas_call(
        finish,
        out_shape=(
            jax.ShapeDtypeStruct((cols, rows), BF16),
            jax.ShapeDtypeStruct((block, cols), F32),
            jax.ShapeDtypeStruct((2,), F32),
        ),
        in_specs=[vmem, vmem, smem, vmem],
        out_specs=(vmem, vmem, smem),
    )(summed, combined, norms, momentum)


def solution(mesh):
    return jax.shard_map(
        body,
        mesh=mesh,
        in_specs=(P("dp", None), P(None, "tensor"), P("dp", "tensor"), P("dp", "tensor")),
        out_specs=(P("tensor", "dp"), P("dp", "tensor"), P()),
        check_vma=False,
    )
```

```python
import functools
import math

import jax
import jax.numpy as jnp
from jax import lax
from jax.experimental import pallas as pl
from jax.experimental.pallas import tpu as pltpu
from jax.sharding import PartitionSpec as P

MESH = pl.DeviceIdType.MESH
NZ, NY, NX, NC = 8, 4, 4, 2
NT = NX * NC
F32, BF16 = jnp.float32, jnp.bfloat16
KCHUNKS = 4
YPAIRS = [(i, j) for i in range(NY) for j in range(i, NY)]
ZPAIRS = [(i, j) for i in range(NZ) for j in range(i, NZ)]


def tree(gram, pairs):
    count = max(j for _, j in pairs) + 1
    value = {}
    for at, (i, j) in enumerate(pairs):
        value[i, j] = value[j, i] = gram[at]
    items = [{i: None} for i in range(count)]

    def weighted(term, coefficient):
        return term if coefficient is None else term * coefficient

    def inner(first, second):
        total = None
        for i, a in first.items():
            for j, c in second.items():
                term = weighted(weighted(value[i, j], a), c)
                total = term if total is None else total + term
        return total

    while len(items) > 1:
        merged = []
        for at in range(0, len(items), 2):
            first, second = items[at], items[at + 1]
            cross, first_sq, second_sq = inner(first, second), inner(first, first), inner(second, second)
            left = 1.0 - cross / (2.0 * first_sq)
            right = 1.0 - cross / (2.0 * second_sq)
            item = {i: weighted(left, a) for i, a in first.items()}
            item.update({i: weighted(right, c) for i, c in second.items()})
            merged.append(item)
        items = merged
    return [items[0][i] for i in range(count)], first_sq, second_sq


def kernel(
    inputs, weight, targets,
    ig_out, comb_out, norm_out,
    ig, comb, norm, gacc,
    xin, w, tg, acc, gin, et, psend, precv, ppart, qin, xrecv, gbuf, zsend, zrecv,
    gsum, red, zred, mine,
    ld_sem, out_sem, own_sem, iy_send, iy_recv, ix_send, ix_recv, is_send, is_recv,
    e_send, e_recv, p_send, p_recv, q_send, q_recv, z_send, z_recv, r_send, r_recv,
):
    dp, t = lax.axis_index("dp"), lax.axis_index("tensor")
    z, y, x, c = dp // NY, dp % NY, t // NC, t % NC
    rows, width = inputs.shape
    cols = weight.shape[1]
    kc = width // KCHUNKS
    part_rows = rows // NT
    block = width // (NZ * NY)
    wide = block * NZ

    def at(dz=0, dy=0, dt=None):
        return ((z + dz) % NZ * NY + (y + dy) % NY, t if dt is None else (t + dt) % NT)

    def at_x(dx, core):
        return (dp, (x + dx) % NX * NC + core)

    loads = []
    for i in range(KCHUNKS):
        a = pltpu.make_async_copy(inputs.at[:, i * kc:(i + 1) * kc], xin.at[:, i * kc:(i + 1) * kc], ld_sem.at[2 * i])
        b = pltpu.make_async_copy(weight.at[i * kc:(i + 1) * kc], w.at[i * kc:(i + 1) * kc], ld_sem.at[2 * i + 1])
        a.start()
        b.start()
        loads.append((a, b))
    tg_load = pltpu.make_async_copy(targets, tg, ld_sem.at[2 * KCHUNKS])
    tg_load.start()

    barrier = pltpu.get_barrier_semaphore()
    line = [at(dz=k) for k in (4, 3, 5, 2, 6, 1, 7)]
    plane = [
        (z * NY + (y + dy) % NY, (x + dx) % NX * NC + (c + dc) % NC)
        for dx in (2, 1, 3, 0) for dy in (2, 1, 3, 0) for dc in range(NC) if dx or dy or dc
    ]
    peers = line + plane
    for peer in peers:
        pl.semaphore_signal(barrier, inc=1, device_id=peer, device_id_type=MESH)
    pl.semaphore_wait(barrier, len(peers))

    def remote(src, dst, send, recv, peer):
        return pltpu.make_async_remote_copy(
            src_ref=src, dst_ref=dst, send_sem=send, recv_sem=recv, device_id=peer, device_id_type=MESH
        )

    my_rows = pl.ds(pl.multiple_of(t * part_rows, part_rows), part_rows)
    for k in (1, 3, 2):
        for b in range(NZ):
            col = pl.multiple_of((b * NY + (y + k) % NY) * block, block)
            remote(
                inputs.at[my_rows, pl.ds(col, block)], gin.at[y, my_rows, b * block:(b + 1) * block],
                iy_send.at[k - 1], iy_recv.at[3 - k], at(dy=k),
            ).start()
    for b in range(NZ):
        col = pl.multiple_of((b * NY + y) * block, block)
        pltpu.make_async_copy(inputs.at[:, pl.ds(col, block)], gin.at[y, :, b * block:(b + 1) * block], own_sem).start()

    for i, (a, b) in enumerate(loads):
        a.wait()
        b.wait()
        part = jnp.dot(xin[:, i * kc:(i + 1) * kc], w[i * kc:(i + 1) * kc, :], preferred_element_type=F32)
        if i == 0:
            acc[...] = part
        else:
            acc[...] += part
    tg_load.wait()
    et[y] = jnp.transpose((acc[...] - tg[...].astype(F32)).astype(BF16))

    half = cols // 2
    low, high = pl.ds(0, half), pl.ds(half, half)
    right, left, across = (y + 1) % NY, (y + 3) % NY, (y + 2) % NY

    def send_error(index, sem, part, dy):
        copy = remote(et.at[index, part], et.at[index, part], e_send.at[sem], e_recv.at[sem], at(dy=dy))
        copy.start()
        return copy

    e_copies = [
        send_error(y, 0, low, 3),
        send_error(y, 3, high, 1),
        send_error(y, 1, high, 3),
        send_error(y, 2, low, 1),
    ]

    def e_wait(index, sem, part):
        remote(et.at[index, part], et.at[index, part], e_send.at[sem], e_recv.at[sem], at(dy=1)).wait_recv()

    sib = at_x(0, 1 - c)
    def rows_of(dx, core):
        return pl.multiple_of(((x + dx) % NX * NC + core) * part_rows, part_rows)

    sub = part_rows // 2
    copies = []

    def share(k, start, count, sends, recvs, sem, peer):
        ref = gin.at[(y + k) % NY, pl.ds(start, count)]
        copy = remote(ref, ref, sends.at[sem], recvs.at[sem], peer)
        copy.start()
        copies.append(copy)

    def shared(k, start, count, sends, recvs, sem):
        ref = gin.at[(y + k) % NY, pl.ds(start, count)]
        remote(ref, ref, sends.at[sem], recvs.at[sem], sib).wait_recv()

    mine_low = rows_of(0, c)
    mine_high = mine_low + sub
    right_low = rows_of(1, c)
    left_low = rows_of(3, c)
    across_low = rows_of(2, c)
    order = (1, 3, 2)
    for k in order:
        ref = gin.at[(y + k) % NY, my_rows]
        remote(ref, ref, iy_send.at[k - 1], iy_recv.at[k - 1], at(dy=k)).wait_recv()
        share(k, mine_low, sub, ix_send, ix_recv, k - 1, at_x(3, c))
        share(k, mine_high, sub, ix_send, ix_recv, 6 + k - 1, at_x(1, c))
        share(k, mine_high, sub, ix_send, ix_recv, 3 + k - 1, at_x(3, c))
        share(k, mine_low, sub, ix_send, ix_recv, 9 + k - 1, at_x(1, c))
        share(k, mine_low, part_rows, is_send, is_recv, k - 1, sib)

    p_copies = []
    for j in range(NX):
        start = pl.multiple_of(((x + j) % NX * NC + 1 - c) * cols, cols)
        psend[j] = jnp.dot(w[pl.ds(start, cols), :], et[y], preferred_element_type=F32).astype(BF16)
        copy = remote(psend.at[j], precv.at[j], p_send.at[j], p_recv.at[j], sib)
        copy.start()
        p_copies.append(copy)
    for j in range(NX):
        start = pl.multiple_of(((x + j) % NX * NC + c) * cols, cols)
        ppart[j] = jnp.dot(w[pl.ds(start, cols), :], et[y], preferred_element_type=F32).astype(BF16)

    def gradient(index):
        gbuf[index] = jnp.dot(et[index], gin[index], preferred_element_type=F32)

    pltpu.make_async_copy(gin.at[y], gin.at[y], own_sem).wait()
    gradient(y)

    for k in order:
        shared(k, right_low, sub, ix_send, ix_recv, k - 1)
        share(k, right_low, sub, ix_send, ix_recv, 12 + k - 1, at_x(3, c))
        shared(k, left_low + sub, sub, ix_send, ix_recv, 6 + k - 1)
        share(k, left_low + sub, sub, ix_send, ix_recv, 15 + k - 1, at_x(1, c))
    e_wait(right, 0, low)
    e_copies.append(send_error(right, 4, low, 3))
    e_wait(left, 3, high)
    e_copies.append(send_error(left, 5, high, 1))
    for j in range(NX):
        p_copies[j].wait_recv()
        ppart[j] = (ppart[j].astype(F32) + precv[j].astype(F32)).astype(BF16)
    for k in order:
        shared(k, right_low + sub, sub, ix_send, ix_recv, 3 + k - 1)
        share(k, right_low, part_rows, is_send, is_recv, 3 + k - 1, sib)
        shared(k, left_low, sub, ix_send, ix_recv, 9 + k - 1)
        share(k, left_low, part_rows, is_send, is_recv, 6 + k - 1, sib)
    for k in order:
        shared(k, across_low, sub, ix_send, ix_recv, 12 + k - 1)
        shared(k, across_low + sub, sub, ix_send, ix_recv, 15 + k - 1)
        share(k, across_low, part_rows, is_send, is_recv, 9 + k - 1, sib)

    def inputs_wait(k):
        for n, dx in enumerate((0, 1, 3, 2)):
            shared(k, rows_of(dx, 1 - c), part_rows, is_send, is_recv, 3 * n + k - 1)

    def fold(value):
        total = value[:, 0:128]
        for l in range(1, value.shape[1] // 128):
            total = total + value[:, l * 128:(l + 1) * 128]
        return total

    zero = jnp.zeros((8, 128), F32)

    def inner_products(items, pairs):
        def step(i, sums):
            at_rows = pl.ds(pl.multiple_of(i * 8, 8), 8)
            values = [gbuf[k, at_rows, :] for k in items]
            return tuple(s + fold(values[a] * values[b]) for s, (a, b) in zip(sums, pairs))

        sums = lax.fori_loop(0, cols // 8, step, (zero,) * len(pairs))
        for value, (a, b) in zip(sums, pairs):
            low_index, high_index = jnp.minimum(items[a], items[b]), jnp.maximum(items[a], items[b])
            gacc[low_index * NY + high_index] = value

    e_wait(right, 1, high)
    inputs_wait(1)
    gradient(right)
    e_wait(left, 2, low)
    inputs_wait(3)
    gradient(left)
    inner_products([y, right, left], [(0, 0), (0, 1), (0, 2), (1, 1), (1, 2), (2, 2)])
    inputs_wait(2)
    e_wait(across, 4, low)
    e_wait(across, 5, high)
    gradient(across)
    inner_products([across, y, right, left], [(0, 0), (0, 1), (0, 2), (0, 3)])

    gsum[...] = jnp.zeros_like(gsum)
    ones = jnp.ones((8, 128), F32)
    lane = lax.broadcasted_iota(jnp.int32, (8, 128), 1)

    def to_lanes(sums):
        for p, value in enumerate(sums):
            gsum[p:p + 1, :] = jnp.sum(value, axis=0, keepdims=True)
        return lax.dot_general(
            ones, gsum[...], (((1,), (1,)), ((), ())), precision=lax.Precision.HIGHEST, preferred_element_type=F32
        )[0:1, :]

    def reduce_stage(value, slot, buffer, me, peers_of):
        mine[slot] = value
        buffer[me] = value
        for peer in peers_of:
            remote(mine.at[slot], buffer.at[me], r_send.at[slot], r_recv.at[slot], peer).start()
        count = len(peers_of)
        some = buffer.at[0:count]
        remote(some, some, r_send.at[slot], r_recv.at[slot], peers_of[0]).wait()
        total = buffer[0]
        for k in range(1, count + 1):
            total = total + buffer[k]
        return total

    def pick(vec, count):
        return [
            jnp.sum(jnp.where(lane[0:1] == p, vec, 0.0), axis=1, keepdims=True) for p in range(count)
        ]

    vec = to_lanes([gacc[a * NY + b] for a, b in YPAIRS])
    vec = reduce_stage(vec, 0, red.at[0], y * NT + t, plane)
    weights, _, _ = tree(pick(vec, len(YPAIRS)), YPAIRS)
    weights = [v * (1.0 / math.sqrt(rows)) for v in weights]

    def combine(b):
        lanes = pl.ds(pl.multiple_of(b * block, block), block)
        total = weights[0] * gbuf[0, :, lanes]
        for k in range(1, NY):
            total = total + weights[k] * gbuf[k, :, lanes]
        return total.astype(BF16)

    z_copies = []
    for k in (4, 3, 5, 2, 6, 1, 7):
        b = (z + k) % NZ
        zsend[k - 1] = combine(b)
        copy = remote(zsend.at[k - 1], zrecv.at[z], z_send.at[k - 1], z_recv.at[NZ - 1 - k], at(dz=k))
        copy.start()
        z_copies.append(copy)
    zrecv[z] = combine(z)

    q_copies = []

    def send_block(src, dst, sem, dx):
        copy = remote(src, dst, q_send.at[sem], q_recv.at[sem], at_x(dx, c))
        copy.start()
        q_copies.append(copy)

    send_block(ppart.at[2, low], qin.at[0], 0, 1)
    send_block(ppart.at[2, high], qin.at[1], 1, 3)
    send_block(ppart.at[1, high], xrecv.at[0, high], 2, 1)
    send_block(ppart.at[3, low], xrecv.at[1, low], 3, 3)
    for k in (1, 2, 3):
        ref = gin.at[(y + k) % NY, my_rows]
        remote(ref, ref, iy_send.at[k - 1], iy_recv.at[k - 1], at(dy=k)).wait_send()
    for copy in e_copies + copies + p_copies:
        copy.wait_send()
    q_copies[0].wait_recv()
    ppart[1, 0:half] = (ppart[1, 0:half].astype(F32) + qin[0].astype(F32)).astype(BF16)
    send_block(ppart.at[1, low], xrecv.at[0, low], 4, 1)
    q_copies[1].wait_recv()
    ppart[3, half:] = (ppart[3, half:].astype(F32) + qin[1].astype(F32)).astype(BF16)
    send_block(ppart.at[3, high], xrecv.at[1, high], 5, 3)
    for copy in q_copies[2:]:
        copy.wait_recv()
    ig[...] = (ppart[0].astype(F32) + (xrecv[0].astype(F32) + xrecv[1].astype(F32))).astype(BF16)
    ig_copy = pltpu.make_async_copy(ig, ig_out, out_sem.at[0])
    ig_copy.start()
    for copy in q_copies:
        copy.wait_send()

    for k in range(1, NZ):
        remote(zrecv.at[(z + k) % NZ], zrecv.at[(z + k) % NZ], z_send.at[k - 1], z_recv.at[k - 1], at(dz=1)).wait_recv()

    def z_step(i, sums):
        at_rows = pl.ds(pl.multiple_of(i * 16, 16), 16)
        items = [zrecv[k, at_rows, :].astype(F32) for k in range(NZ)]
        out = []
        for s, (a, b) in zip(sums, ZPAIRS):
            product = items[a] * items[b]
            out.append(s + product[0:8] + product[8:16])
        return tuple(out)

    vec = to_lanes(lax.fori_loop(0, cols // 16, z_step, (zero,) * len(ZPAIRS)))
    vec = reduce_stage(vec, 1, zred, z, line)
    vec = reduce_stage(vec, 2, red.at[1], y * NT + t, plane)
    weights, first_sq, second_sq = tree(pick(vec, len(ZPAIRS)), ZPAIRS)
    total = weights[0] * zrecv[0].astype(F32)
    for k in range(1, NZ):
        total = total + weights[k] * zrecv[k].astype(F32)
    comb[...] = jnp.transpose(total)
    comb_copy = pltpu.make_async_copy(comb, comb_out, out_sem.at[1])
    comb_copy.start()
    norm[...] = jnp.where(lane[0:1] == 0, jnp.sqrt(first_sq), jnp.sqrt(second_sq)) * (1.0 / width)
    norm_copy = pltpu.make_async_copy(norm, norm_out, out_sem.at[2])
    norm_copy.start()
    for copy in z_copies:
        copy.wait_send()
    ig_copy.wait()
    comb_copy.wait()
    norm_copy.wait()


def finish(ig, comb, norm, momentum, ig_out, momentum_out, norm_out):
    ig_out[...] = ig[...]
    momentum_out[...] = 0.9 * momentum[...] + comb[...]
    norm_out[0] = norm[0, 0]
    norm_out[1] = norm[0, 1]


def body(inputs, weight, targets, momentum):
    rows, width = inputs.shape
    cols = weight.shape[1]
    block = width // (NZ * NY)
    wide = block * NZ
    dma = pltpu.SemaphoreType.DMA
    any_spec = pl.BlockSpec(memory_space=pl.ANY)
    vmem = pl.BlockSpec(memory_space=pltpu.VMEM)
    summed, combined, norms = pl.pallas_call(
        kernel,
        out_shape=(
            jax.ShapeDtypeStruct((cols, rows), BF16),
            jax.ShapeDtypeStruct((block, cols), F32),
            jax.ShapeDtypeStruct((1, 128), F32),
        ),
        in_specs=[any_spec] * 3,
        out_specs=(any_spec,) * 3,
        scratch_shapes=[
            pltpu.VMEM((cols, rows), BF16),
            pltpu.VMEM((block, cols), F32),
            pltpu.VMEM((1, 128), F32),
            pltpu.VMEM((NY * NY, 8, 128), F32),
            pltpu.VMEM((rows, width), BF16),
            pltpu.VMEM((width, cols), BF16),
            pltpu.VMEM((rows, cols), BF16),
            pltpu.VMEM((rows, cols), F32),
            pltpu.VMEM((NY, rows, wide), BF16),
            pltpu.VMEM((NY, cols, rows), BF16),
            pltpu.VMEM((NX, cols, rows), BF16),
            pltpu.VMEM((NX, cols, rows), BF16),
            pltpu.VMEM((NX, cols, rows), BF16),
            pltpu.VMEM((2, cols // 2, rows), BF16),
            pltpu.VMEM((2, cols, rows), BF16),
            pltpu.VMEM((NY, cols, wide), F32),
            pltpu.VMEM((NZ - 1, cols, block), BF16),
            pltpu.VMEM((NZ, cols, block), BF16),
            pltpu.VMEM((128, 128), F32),
            pltpu.VMEM((2, NY * NT, 1, 128), F32),
            pltpu.VMEM((NZ, 1, 128), F32),
            pltpu.VMEM((3, 1, 128), F32),
            dma((2 * KCHUNKS + 1,)),
            dma((3,)),
            dma,
            dma((3,)), dma((3,)),
            dma((18,)), dma((18,)),
            dma((12,)), dma((12,)),
            dma((6,)), dma((6,)),
            dma((NX,)), dma((NX,)),
            dma((6,)), dma((6,)),
            dma((NZ - 1,)), dma((NZ - 1,)),
            dma((3,)), dma((3,)),
        ],
        compiler_params=pltpu.CompilerParams(
            collective_id=0, has_side_effects=True, vmem_limit_bytes=53 * 2**20
        ),
    )(inputs, weight, targets)
    smem = pl.BlockSpec(memory_space=pltpu.SMEM)
    return pl.pallas_call(
        finish,
        out_shape=(
            jax.ShapeDtypeStruct((cols, rows), BF16),
            jax.ShapeDtypeStruct((block, cols), F32),
            jax.ShapeDtypeStruct((2,), F32),
        ),
        in_specs=[vmem, vmem, smem, vmem],
        out_specs=(vmem, vmem, smem),
        compiler_params=pltpu.CompilerParams(vmem_limit_bytes=4 * 2**20),
    )(summed, combined, norms, momentum)


def solution(mesh):
    return jax.shard_map(
        body,
        mesh=mesh,
        in_specs=(P("dp", None), P(None, "tensor"), P("dp", "tensor"), P("dp", "tensor")),
        out_specs=(P("tensor", "dp"), P("dp", "tensor"), P()),
        check_vma=False,
    )
```

```python
import functools
import math

import jax
import jax.numpy as jnp
from jax import lax
from jax.experimental import pallas as pl
from jax.experimental.pallas import tpu as pltpu
from jax.sharding import PartitionSpec as P

MESH = pl.DeviceIdType.MESH
NZ, NY, NX, NC = 8, 4, 4, 2
NT = NX * NC
F32, BF16 = jnp.float32, jnp.bfloat16
KCHUNKS = 4
YPAIRS = [(i, j) for i in range(NY) for j in range(i, NY)]
ZPAIRS = [(i, j) for i in range(NZ) for j in range(i, NZ)]


def tree(gram, pairs):
    count = max(j for _, j in pairs) + 1
    value = {}
    for at, (i, j) in enumerate(pairs):
        value[i, j] = value[j, i] = gram[at]
    items = [{i: None} for i in range(count)]

    def weighted(term, coefficient):
        return term if coefficient is None else term * coefficient

    def inner(first, second):
        total = None
        for i, a in first.items():
            for j, c in second.items():
                term = weighted(weighted(value[i, j], a), c)
                total = term if total is None else total + term
        return total

    while len(items) > 1:
        merged = []
        for at in range(0, len(items), 2):
            first, second = items[at], items[at + 1]
            cross, first_sq, second_sq = inner(first, second), inner(first, first), inner(second, second)
            left = 1.0 - cross / (2.0 * first_sq)
            right = 1.0 - cross / (2.0 * second_sq)
            item = {i: weighted(left, a) for i, a in first.items()}
            item.update({i: weighted(right, c) for i, c in second.items()})
            merged.append(item)
        items = merged
    return [items[0][i] for i in range(count)], first_sq, second_sq


def kernel(
    inputs, weight, targets,
    ig_out, comb_out, norm_out,
    ig, comb, norm, gacc, zacc,
    xin, w, tg, acc, gin, et, psend, precv, ppart, qin, xrecv, gbuf, zsend, zrecv,
    gsum, red, zred, mine,
    ld_sem, out_sem, own_sem, iy_send, iy_recv, ix_send, ix_recv, is_send, is_recv,
    e_send, e_recv, p_send, p_recv, q_send, q_recv, z_send, z_recv, r_send, r_recv,
):
    dp, t = lax.axis_index("dp"), lax.axis_index("tensor")
    z, y, x, c = dp // NY, dp % NY, t // NC, t % NC
    rows, width = inputs.shape
    cols = weight.shape[1]
    kc = width // KCHUNKS
    part_rows = rows // NT
    block = width // (NZ * NY)
    wide = block * NZ

    def at(dz=0, dy=0, dt=None):
        return ((z + dz) % NZ * NY + (y + dy) % NY, t if dt is None else (t + dt) % NT)

    def at_x(dx, core):
        return (dp, (x + dx) % NX * NC + core)

    barrier = pltpu.get_barrier_semaphore()
    line = [at(dz=k) for k in (4, 3, 5, 2, 6, 1, 7)]
    plane = [
        (z * NY + (y + dy) % NY, (x + dx) % NX * NC + (c + dc) % NC)
        for dx in (2, 1, 3, 0) for dy in (2, 1, 3, 0) for dc in range(NC) if dx or dy or dc
    ]
    peers = line + plane
    for peer in peers:
        pl.semaphore_signal(barrier, inc=1, device_id=peer, device_id_type=MESH)
    loads = []
    for i in range(KCHUNKS):
        a = pltpu.make_async_copy(inputs.at[:, i * kc:(i + 1) * kc], xin.at[:, i * kc:(i + 1) * kc], ld_sem.at[2 * i])
        b = pltpu.make_async_copy(weight.at[i * kc:(i + 1) * kc], w.at[i * kc:(i + 1) * kc], ld_sem.at[2 * i + 1])
        a.start()
        b.start()
        loads.append((a, b))
    tg_load = pltpu.make_async_copy(targets, tg, ld_sem.at[2 * KCHUNKS])
    tg_load.start()

    pl.semaphore_wait(barrier, len(peers))

    def remote(src, dst, send, recv, peer):
        return pltpu.make_async_remote_copy(
            src_ref=src, dst_ref=dst, send_sem=send, recv_sem=recv, device_id=peer, device_id_type=MESH
        )

    my_rows = pl.ds(pl.multiple_of(t * part_rows, part_rows), part_rows)
    for k in (1, 3, 2):
        for b in range(NZ):
            col = pl.multiple_of((b * NY + (y + k) % NY) * block, block)
            remote(
                inputs.at[my_rows, pl.ds(col, block)], gin.at[y, my_rows, b * block:(b + 1) * block],
                iy_send.at[k - 1], iy_recv.at[3 - k], at(dy=k),
            ).start()
    for b in range(NZ):
        col = pl.multiple_of((b * NY + y) * block, block)
        pltpu.make_async_copy(inputs.at[:, pl.ds(col, block)], gin.at[y, :, b * block:(b + 1) * block], own_sem).start()

    for i, (a, b) in enumerate(loads):
        a.wait()
        b.wait()
        part = jnp.dot(xin[:, i * kc:(i + 1) * kc], w[i * kc:(i + 1) * kc, :], preferred_element_type=F32)
        if i == 0:
            acc[...] = part
        else:
            acc[...] += part
    tg_load.wait()
    et[y] = jnp.transpose((acc[...] - tg[...].astype(F32)).astype(BF16))

    half = cols // 2
    low, high = pl.ds(0, half), pl.ds(half, half)
    right, left, across = (y + 1) % NY, (y + 3) % NY, (y + 2) % NY

    def send_error(index, sem, part, dy):
        copy = remote(et.at[index, part], et.at[index, part], e_send.at[sem], e_recv.at[sem], at(dy=dy))
        copy.start()
        return copy

    e_copies = [
        send_error(y, 0, low, 3),
        send_error(y, 3, high, 1),
        send_error(y, 1, high, 3),
        send_error(y, 2, low, 1),
    ]

    def e_wait(index, sem, part):
        remote(et.at[index, part], et.at[index, part], e_send.at[sem], e_recv.at[sem], at(dy=1)).wait_recv()

    sib = at_x(0, 1 - c)
    def rows_of(dx, core):
        return pl.multiple_of(((x + dx) % NX * NC + core) * part_rows, part_rows)

    sub = part_rows // 2
    copies = []

    def share(k, start, count, sends, recvs, sem, peer):
        ref = gin.at[(y + k) % NY, pl.ds(start, count)]
        copy = remote(ref, ref, sends.at[sem], recvs.at[sem], peer)
        copy.start()
        copies.append(copy)

    def shared(k, start, count, sends, recvs, sem):
        ref = gin.at[(y + k) % NY, pl.ds(start, count)]
        remote(ref, ref, sends.at[sem], recvs.at[sem], sib).wait_recv()

    mine_low = rows_of(0, c)
    mine_high = mine_low + sub
    right_low = rows_of(1, c)
    left_low = rows_of(3, c)
    across_low = rows_of(2, c)
    order = (1, 3, 2)
    for k in order:
        ref = gin.at[(y + k) % NY, my_rows]
        remote(ref, ref, iy_send.at[k - 1], iy_recv.at[k - 1], at(dy=k)).wait_recv()
        share(k, mine_low, sub, ix_send, ix_recv, k - 1, at_x(3, c))
        share(k, mine_high, sub, ix_send, ix_recv, 6 + k - 1, at_x(1, c))
        share(k, mine_high, sub, ix_send, ix_recv, 3 + k - 1, at_x(3, c))
        share(k, mine_low, sub, ix_send, ix_recv, 9 + k - 1, at_x(1, c))
        share(k, mine_low, part_rows, is_send, is_recv, k - 1, sib)

    p_copies = []
    for j in range(NX):
        start = pl.multiple_of(((x + j) % NX * NC + 1 - c) * cols, cols)
        psend[j] = jnp.dot(w[pl.ds(start, cols), :], et[y], preferred_element_type=F32).astype(BF16)
        copy = remote(psend.at[j], precv.at[j], p_send.at[j], p_recv.at[j], sib)
        copy.start()
        p_copies.append(copy)
    for j in range(NX):
        start = pl.multiple_of(((x + j) % NX * NC + c) * cols, cols)
        ppart[j] = jnp.dot(w[pl.ds(start, cols), :], et[y], preferred_element_type=F32).astype(BF16)

    def gradient(index):
        gbuf[index] = jnp.dot(et[index], gin[index], preferred_element_type=F32)

    pltpu.make_async_copy(gin.at[y], gin.at[y], own_sem).wait()
    gradient(y)

    for k in order:
        shared(k, right_low, sub, ix_send, ix_recv, k - 1)
        share(k, right_low, sub, ix_send, ix_recv, 12 + k - 1, at_x(3, c))
        shared(k, left_low + sub, sub, ix_send, ix_recv, 6 + k - 1)
        share(k, left_low + sub, sub, ix_send, ix_recv, 15 + k - 1, at_x(1, c))
    e_wait(right, 0, low)
    e_copies.append(send_error(right, 4, low, 3))
    e_wait(left, 3, high)
    e_copies.append(send_error(left, 5, high, 1))
    for j in range(NX):
        p_copies[j].wait_recv()
        ppart[j] = (ppart[j].astype(F32) + precv[j].astype(F32)).astype(BF16)
    for k in order:
        shared(k, right_low + sub, sub, ix_send, ix_recv, 3 + k - 1)
        share(k, right_low, part_rows, is_send, is_recv, 3 + k - 1, sib)
        shared(k, left_low, sub, ix_send, ix_recv, 9 + k - 1)
        share(k, left_low, part_rows, is_send, is_recv, 6 + k - 1, sib)
    for k in order:
        shared(k, across_low, sub, ix_send, ix_recv, 12 + k - 1)
        shared(k, across_low + sub, sub, ix_send, ix_recv, 15 + k - 1)
        share(k, across_low, part_rows, is_send, is_recv, 9 + k - 1, sib)

    def inputs_wait(k):
        for n, dx in enumerate((0, 1, 3, 2)):
            shared(k, rows_of(dx, 1 - c), part_rows, is_send, is_recv, 3 * n + k - 1)

    def fold(value):
        total = value[:, 0:128]
        for l in range(1, value.shape[1] // 128):
            total = total + value[:, l * 128:(l + 1) * 128]
        return total

    zero = jnp.zeros((8, 128), F32)

    def inner_products(items, pairs):
        def step(i, sums):
            at_rows = pl.ds(pl.multiple_of(i * 8, 8), 8)
            values = [gbuf[k, at_rows, :] for k in items]
            return tuple(s + fold(values[a] * values[b]) for s, (a, b) in zip(sums, pairs))

        sums = lax.fori_loop(0, cols // 8, step, (zero,) * len(pairs), unroll=4)
        for value, (a, b) in zip(sums, pairs):
            low_index, high_index = jnp.minimum(items[a], items[b]), jnp.maximum(items[a], items[b])
            gacc[low_index * NY + high_index] = value

    e_wait(right, 1, high)
    inputs_wait(1)
    gradient(right)
    e_wait(left, 2, low)
    inputs_wait(3)
    gradient(left)
    inner_products([y, right, left], [(0, 0), (0, 1), (0, 2), (1, 1), (1, 2), (2, 2)])
    inputs_wait(2)
    e_wait(across, 4, low)
    e_wait(across, 5, high)
    gradient(across)
    inner_products([across, y, right, left], [(0, 0), (0, 1), (0, 2), (0, 3)])

    gsum[...] = jnp.zeros_like(gsum)
    ones = jnp.ones((8, 128), F32)
    lane = lax.broadcasted_iota(jnp.int32, (8, 128), 1)

    def to_lanes(sums):
        for p, value in enumerate(sums):
            gsum[p:p + 1, :] = jnp.sum(value, axis=0, keepdims=True)
        return lax.dot_general(
            ones, gsum[...], (((1,), (1,)), ((), ())), precision=lax.Precision.HIGHEST, preferred_element_type=F32
        )[0:1, :]

    def reduce_stage(value, slot, buffer, me, peers_of):
        mine[slot] = value
        buffer[me] = value
        for peer in peers_of:
            remote(mine.at[slot], buffer.at[me], r_send.at[slot], r_recv.at[slot], peer).start()
        count = len(peers_of)
        some = buffer.at[0:count]
        remote(some, some, r_send.at[slot], r_recv.at[slot], peers_of[0]).wait()
        total = buffer[0]
        for k in range(1, count + 1):
            total = total + buffer[k]
        return total

    def pick(vec, count):
        return [
            jnp.sum(jnp.where(lane[0:1] == p, vec, 0.0), axis=1, keepdims=True) for p in range(count)
        ]

    vec = to_lanes([gacc[a * NY + b] for a, b in YPAIRS])
    vec = reduce_stage(vec, 0, red.at[0], y * NT + t, plane)
    weights, _, _ = tree(pick(vec, len(YPAIRS)), YPAIRS)
    weights = [v * (1.0 / math.sqrt(rows)) for v in weights]

    def combine(b):
        lanes = pl.ds(pl.multiple_of(b * block, block), block)
        total = weights[0] * gbuf[0, :, lanes]
        for k in range(1, NY):
            total = total + weights[k] * gbuf[k, :, lanes]
        return total.astype(BF16)

    z_copies = []
    for k in (4, 3, 5, 2, 6, 1, 7):
        b = (z + k) % NZ
        zsend[k - 1] = combine(b)
        copy = remote(zsend.at[k - 1], zrecv.at[z], z_send.at[k - 1], z_recv.at[NZ - 1 - k], at(dz=k))
        copy.start()
        z_copies.append(copy)
    zrecv[z] = combine(z)

    q_copies = []

    def send_block(src, dst, sem, dx):
        copy = remote(src, dst, q_send.at[sem], q_recv.at[sem], at_x(dx, c))
        copy.start()
        q_copies.append(copy)

    send_block(ppart.at[2, low], qin.at[0], 0, 1)
    send_block(ppart.at[2, high], qin.at[1], 1, 3)
    send_block(ppart.at[1, high], xrecv.at[0, high], 2, 1)
    send_block(ppart.at[3, low], xrecv.at[1, low], 3, 3)
    for k in (1, 2, 3):
        ref = gin.at[(y + k) % NY, my_rows]
        remote(ref, ref, iy_send.at[k - 1], iy_recv.at[k - 1], at(dy=k)).wait_send()
    for copy in e_copies + copies + p_copies:
        copy.wait_send()
    q_copies[0].wait_recv()
    ppart[1, 0:half] = (ppart[1, 0:half].astype(F32) + qin[0].astype(F32)).astype(BF16)
    send_block(ppart.at[1, low], xrecv.at[0, low], 4, 1)
    q_copies[1].wait_recv()
    ppart[3, half:] = (ppart[3, half:].astype(F32) + qin[1].astype(F32)).astype(BF16)
    send_block(ppart.at[3, high], xrecv.at[1, high], 5, 3)
    for copy in q_copies[2:]:
        copy.wait_recv()
    ig[...] = (ppart[0].astype(F32) + (xrecv[0].astype(F32) + xrecv[1].astype(F32))).astype(BF16)
    ig_copy = pltpu.make_async_copy(ig, ig_out, out_sem.at[0])
    ig_copy.start()
    for copy in q_copies:
        copy.wait_send()

    def z_wait(k):
        ref = zrecv.at[(z + k) % NZ]
        remote(ref, ref, z_send.at[k - 1], z_recv.at[k - 1], at(dz=1)).wait_recv()

    def z_products(items, pairs):
        def step(i, sums):
            at_rows = pl.ds(pl.multiple_of(i * 16, 16), 16)
            values = [zrecv[k, at_rows, :].astype(F32) for k in items]
            out = []
            for s, (a, b) in zip(sums, pairs):
                product = values[a] * values[b]
                out.append(s + (product[0:8] + product[8:16]))
            return tuple(out)

        sums = lax.fori_loop(0, cols // 16, step, (zero,) * len(pairs), unroll=2)
        for value, (a, b) in zip(sums, pairs):
            low_index, high_index = jnp.minimum(items[a], items[b]), jnp.maximum(items[a], items[b])
            zacc[low_index * NZ + high_index] = value

    late, early = (7, 1), (4, 3, 5, 2, 6)
    for k in early:
        z_wait(k)
    items = [(z + k) % NZ for k in late + early + (0,)]
    z_products(items[2:], [(a, b) for a in range(6) for b in range(a, 6)])
    for k in late:
        z_wait(k)
    z_products(items, [(a, b) for a in range(2) for b in range(a, NZ)])
    vec = to_lanes([zacc[a * NZ + b] for a, b in ZPAIRS])
    vec = reduce_stage(vec, 1, zred, z, line)
    vec = reduce_stage(vec, 2, red.at[1], y * NT + t, plane)
    weights, first_sq, second_sq = tree(pick(vec, len(ZPAIRS)), ZPAIRS)
    total = weights[0] * zrecv[0].astype(F32)
    for k in range(1, NZ):
        total = total + weights[k] * zrecv[k].astype(F32)
    comb_out[...] = jnp.transpose(total)
    norm_out[...] = jnp.where(lane[0:1] == 0, jnp.sqrt(first_sq), jnp.sqrt(second_sq)) * (1.0 / width)
    for copy in z_copies:
        copy.wait_send()
    ig_copy.wait()


def finish(ig, comb, norm, momentum, ig_out, momentum_out, norm_out):
    ig_out[...] = ig[...]
    momentum_out[...] = 0.9 * momentum[...] + comb[...]
    norm_out[0] = norm[0, 0]
    norm_out[1] = norm[0, 1]


def body(inputs, weight, targets, momentum):
    rows, width = inputs.shape
    cols = weight.shape[1]
    block = width // (NZ * NY)
    wide = block * NZ
    dma = pltpu.SemaphoreType.DMA
    any_spec = pl.BlockSpec(memory_space=pl.ANY)
    vmem = pl.BlockSpec(memory_space=pltpu.VMEM)
    summed, combined, norms = pl.pallas_call(
        kernel,
        out_shape=(
            jax.ShapeDtypeStruct((cols, rows), BF16),
            jax.ShapeDtypeStruct((block, cols), F32),
            jax.ShapeDtypeStruct((1, 128), F32),
        ),
        in_specs=[any_spec] * 3,
        out_specs=(any_spec, vmem, vmem),
        scratch_shapes=[
            pltpu.VMEM((cols, rows), BF16),
            pltpu.VMEM((block, cols), F32),
            pltpu.VMEM((1, 128), F32),
            pltpu.VMEM((NY * NY, 8, 128), F32),
            pltpu.VMEM((NZ * NZ, 8, 128), F32),
            pltpu.VMEM((rows, width), BF16),
            pltpu.VMEM((width, cols), BF16),
            pltpu.VMEM((rows, cols), BF16),
            pltpu.VMEM((rows, cols), F32),
            pltpu.VMEM((NY, rows, wide), BF16),
            pltpu.VMEM((NY, cols, rows), BF16),
            pltpu.VMEM((NX, cols, rows), BF16),
            pltpu.VMEM((NX, cols, rows), BF16),
            pltpu.VMEM((NX, cols, rows), BF16),
            pltpu.VMEM((2, cols // 2, rows), BF16),
            pltpu.VMEM((2, cols, rows), BF16),
            pltpu.VMEM((NY, cols, wide), F32),
            pltpu.VMEM((NZ - 1, cols, block), BF16),
            pltpu.VMEM((NZ, cols, block), BF16),
            pltpu.VMEM((128, 128), F32),
            pltpu.VMEM((2, NY * NT, 1, 128), F32),
            pltpu.VMEM((NZ, 1, 128), F32),
            pltpu.VMEM((3, 1, 128), F32),
            dma((2 * KCHUNKS + 1,)),
            dma((3,)),
            dma,
            dma((3,)), dma((3,)),
            dma((18,)), dma((18,)),
            dma((12,)), dma((12,)),
            dma((6,)), dma((6,)),
            dma((NX,)), dma((NX,)),
            dma((6,)), dma((6,)),
            dma((NZ - 1,)), dma((NZ - 1,)),
            dma((3,)), dma((3,)),
        ],
        compiler_params=pltpu.CompilerParams(
            collective_id=0, has_side_effects=True, vmem_limit_bytes=53 * 2**20
        ),
    )(inputs, weight, targets)
    smem = pl.BlockSpec(memory_space=pltpu.SMEM)
    return pl.pallas_call(
        finish,
        out_shape=(
            jax.ShapeDtypeStruct((cols, rows), BF16),
            jax.ShapeDtypeStruct((block, cols), F32),
            jax.ShapeDtypeStruct((2,), F32),
        ),
        in_specs=[vmem, vmem, smem, vmem],
        out_specs=(vmem, vmem, smem),
        compiler_params=pltpu.CompilerParams(vmem_limit_bytes=4 * 2**20),
    )(summed, combined, norms, momentum)


def solution(mesh):
    return jax.shard_map(
        body,
        mesh=mesh,
        in_specs=(P("dp", None), P(None, "tensor"), P("dp", "tensor"), P("dp", "tensor")),
        out_specs=(P("tensor", "dp"), P("dp", "tensor"), P()),
        check_vma=False,
    )
```

```python
import functools
import math

import jax
import jax.numpy as jnp
from jax import lax
from jax.experimental import pallas as pl
from jax.experimental.pallas import tpu as pltpu
from jax.sharding import PartitionSpec as P

MESH = pl.DeviceIdType.MESH
NZ, NY, NX, NC = 8, 4, 4, 2
NT = NX * NC
F32, BF16 = jnp.float32, jnp.bfloat16
KCHUNKS = 4
YPAIRS = [(i, j) for i in range(NY) for j in range(i, NY)]
ZPAIRS = [(i, j) for i in range(NZ) for j in range(i, NZ)]


def tree(gram, pairs):
    count = max(j for _, j in pairs) + 1
    value = {}
    for at, (i, j) in enumerate(pairs):
        value[i, j] = value[j, i] = gram[at]
    items = [{i: None} for i in range(count)]

    def weighted(term, coefficient):
        return term if coefficient is None else term * coefficient

    def inner(first, second):
        total = None
        for i, a in first.items():
            for j, c in second.items():
                term = weighted(weighted(value[i, j], a), c)
                total = term if total is None else total + term
        return total

    while len(items) > 1:
        merged = []
        for at in range(0, len(items), 2):
            first, second = items[at], items[at + 1]
            cross, first_sq, second_sq = inner(first, second), inner(first, first), inner(second, second)
            left = 1.0 - cross / (2.0 * first_sq)
            right = 1.0 - cross / (2.0 * second_sq)
            item = {i: weighted(left, a) for i, a in first.items()}
            item.update({i: weighted(right, c) for i, c in second.items()})
            merged.append(item)
        items = merged
    return [items[0][i] for i in range(count)], first_sq, second_sq


def kernel(
    inputs, weight, targets,
    ig_out, comb_out, norm_out,
    ig, comb, norm, gacc, zacc,
    xin, w, tg, acc, gin, et, psend, precv, ppart, qin, xrecv, gbuf, zsend, zrecv,
    gsum, red, zred, mine,
    ld_sem, out_sem, own_sem, iy_send, iy_recv, ix_send, ix_recv, is_send, is_recv,
    e_send, e_recv, p_send, p_recv, q_send, q_recv, z_send, z_recv, r_send, r_recv,
):
    dp, t = lax.axis_index("dp"), lax.axis_index("tensor")
    z, y, x, c = dp // NY, dp % NY, t // NC, t % NC
    rows, width = inputs.shape
    cols = weight.shape[1]
    kc = width // KCHUNKS
    part_rows = rows // NT
    block = width // (NZ * NY)
    wide = block * NZ

    def at(dz=0, dy=0, dt=None):
        return ((z + dz) % NZ * NY + (y + dy) % NY, t if dt is None else (t + dt) % NT)

    def at_x(dx, core):
        return (dp, (x + dx) % NX * NC + core)

    barrier = pltpu.get_barrier_semaphore()
    line = [at(dz=k) for k in (4, 3, 5, 2, 6, 1, 7)]
    plane = [
        (z * NY + (y + dy) % NY, (x + dx) % NX * NC + (c + dc) % NC)
        for dx in (2, 1, 3, 0) for dy in (2, 1, 3, 0) for dc in range(NC) if dx or dy or dc
    ]
    peers = line + plane
    for peer in peers:
        pl.semaphore_signal(barrier, inc=1, device_id=peer, device_id_type=MESH)
    loads = []
    for i in range(KCHUNKS):
        a = pltpu.make_async_copy(inputs.at[:, i * kc:(i + 1) * kc], xin.at[:, i * kc:(i + 1) * kc], ld_sem.at[2 * i])
        b = pltpu.make_async_copy(weight.at[i * kc:(i + 1) * kc], w.at[i * kc:(i + 1) * kc], ld_sem.at[2 * i + 1])
        a.start()
        b.start()
        loads.append((a, b))
    tg_load = pltpu.make_async_copy(targets, tg, ld_sem.at[2 * KCHUNKS])
    tg_load.start()

    pl.semaphore_wait(barrier, len(peers))

    def remote(src, dst, send, recv, peer):
        return pltpu.make_async_remote_copy(
            src_ref=src, dst_ref=dst, send_sem=send, recv_sem=recv, device_id=peer, device_id_type=MESH
        )

    my_rows = pl.ds(pl.multiple_of(t * part_rows, part_rows), part_rows)
    for k in (1, 3, 2):
        for b in range(NZ):
            col = pl.multiple_of((b * NY + (y + k) % NY) * block, block)
            remote(
                inputs.at[my_rows, pl.ds(col, block)], gin.at[y, my_rows, b * block:(b + 1) * block],
                iy_send.at[k - 1], iy_recv.at[3 - k], at(dy=k),
            ).start()
    for b in range(NZ):
        col = pl.multiple_of((b * NY + y) * block, block)
        pltpu.make_async_copy(inputs.at[:, pl.ds(col, block)], gin.at[y, :, b * block:(b + 1) * block], own_sem).start()

    for i, (a, b) in enumerate(loads):
        a.wait()
        b.wait()
        part = jnp.dot(xin[:, i * kc:(i + 1) * kc], w[i * kc:(i + 1) * kc, :], preferred_element_type=F32)
        if i == 0:
            acc[...] = part
        else:
            acc[...] += part
    tg_load.wait()
    et[y] = jnp.transpose((acc[...] - tg[...].astype(F32)).astype(BF16))

    half = cols // 2
    low, high = pl.ds(0, half), pl.ds(half, half)
    right, left, across = (y + 1) % NY, (y + 3) % NY, (y + 2) % NY

    def send_error(index, sem, part, dy):
        copy = remote(et.at[index, part], et.at[index, part], e_send.at[sem], e_recv.at[sem], at(dy=dy))
        copy.start()
        return copy

    e_copies = [
        send_error(y, 0, low, 3),
        send_error(y, 3, high, 1),
        send_error(y, 1, high, 3),
        send_error(y, 2, low, 1),
    ]

    def e_wait(index, sem, part):
        remote(et.at[index, part], et.at[index, part], e_send.at[sem], e_recv.at[sem], at(dy=1)).wait_recv()

    sib = at_x(0, 1 - c)
    def rows_of(dx, core):
        return pl.multiple_of(((x + dx) % NX * NC + core) * part_rows, part_rows)

    sub = part_rows // 2
    copies = []

    def share(k, start, count, sends, recvs, sem, peer):
        ref = gin.at[(y + k) % NY, pl.ds(start, count)]
        copy = remote(ref, ref, sends.at[sem], recvs.at[sem], peer)
        copy.start()
        copies.append(copy)

    def shared(k, start, count, sends, recvs, sem):
        ref = gin.at[(y + k) % NY, pl.ds(start, count)]
        remote(ref, ref, sends.at[sem], recvs.at[sem], sib).wait_recv()

    mine_low = rows_of(0, c)
    mine_high = mine_low + sub
    right_low = rows_of(1, c)
    left_low = rows_of(3, c)
    across_low = rows_of(2, c)
    order = (1, 3, 2)
    for k in order:
        ref = gin.at[(y + k) % NY, my_rows]
        remote(ref, ref, iy_send.at[k - 1], iy_recv.at[k - 1], at(dy=k)).wait_recv()
        share(k, mine_low, sub, ix_send, ix_recv, k - 1, at_x(3, c))
        share(k, mine_high, sub, ix_send, ix_recv, 6 + k - 1, at_x(1, c))
        share(k, mine_high, sub, ix_send, ix_recv, 3 + k - 1, at_x(3, c))
        share(k, mine_low, sub, ix_send, ix_recv, 9 + k - 1, at_x(1, c))
        share(k, mine_low, part_rows, is_send, is_recv, k - 1, sib)

    p_copies = []
    for j in range(NX):
        start = pl.multiple_of(((x + j) % NX * NC + 1 - c) * cols, cols)
        psend[j] = jnp.dot(w[pl.ds(start, cols), :], et[y], preferred_element_type=F32).astype(BF16)
        copy = remote(psend.at[j], precv.at[j], p_send.at[j], p_recv.at[j], sib)
        copy.start()
        p_copies.append(copy)
    for j in range(NX):
        start = pl.multiple_of(((x + j) % NX * NC + c) * cols, cols)
        ppart[j] = jnp.dot(w[pl.ds(start, cols), :], et[y], preferred_element_type=F32).astype(BF16)

    def gradient(index):
        gbuf[index] = jnp.dot(et[index], gin[index], preferred_element_type=F32)

    pltpu.make_async_copy(gin.at[y], gin.at[y], own_sem).wait()
    gradient(y)

    for k in order:
        shared(k, right_low, sub, ix_send, ix_recv, k - 1)
        share(k, right_low, sub, ix_send, ix_recv, 12 + k - 1, at_x(3, c))
        shared(k, left_low + sub, sub, ix_send, ix_recv, 6 + k - 1)
        share(k, left_low + sub, sub, ix_send, ix_recv, 15 + k - 1, at_x(1, c))
    e_wait(right, 0, low)
    e_copies.append(send_error(right, 4, low, 3))
    e_wait(left, 3, high)
    e_copies.append(send_error(left, 5, high, 1))
    for j in range(NX):
        p_copies[j].wait_recv()
        ppart[j] = (ppart[j].astype(F32) + precv[j].astype(F32)).astype(BF16)
    for k in order:
        shared(k, right_low + sub, sub, ix_send, ix_recv, 3 + k - 1)
        share(k, right_low, part_rows, is_send, is_recv, 3 + k - 1, sib)
        shared(k, left_low, sub, ix_send, ix_recv, 9 + k - 1)
        share(k, left_low, part_rows, is_send, is_recv, 6 + k - 1, sib)
    for k in order:
        shared(k, across_low, sub, ix_send, ix_recv, 12 + k - 1)
        shared(k, across_low + sub, sub, ix_send, ix_recv, 15 + k - 1)
        share(k, across_low, part_rows, is_send, is_recv, 9 + k - 1, sib)

    def inputs_wait(k):
        for n, dx in enumerate((0, 1, 3, 2)):
            shared(k, rows_of(dx, 1 - c), part_rows, is_send, is_recv, 3 * n + k - 1)

    def fold(value):
        total = value[:, 0:128]
        for l in range(1, value.shape[1] // 128):
            total = total + value[:, l * 128:(l + 1) * 128]
        return total

    zero = jnp.zeros((8, 128), F32)

    def inner_products(items, pairs):
        def step(i, sums):
            at_rows = pl.ds(pl.multiple_of(i * 8, 8), 8)
            values = [gbuf[k, at_rows, :] for k in items]
            return tuple(s + fold(values[a] * values[b]) for s, (a, b) in zip(sums, pairs))

        sums = lax.fori_loop(0, cols // 8, step, (zero,) * len(pairs), unroll=4)
        for value, (a, b) in zip(sums, pairs):
            low_index, high_index = jnp.minimum(items[a], items[b]), jnp.maximum(items[a], items[b])
            gacc[low_index * NY + high_index] = value

    e_wait(right, 1, high)
    inputs_wait(1)
    gradient(right)
    e_wait(left, 2, low)
    inputs_wait(3)
    gradient(left)
    inner_products([y, right, left], [(0, 0), (0, 1), (0, 2), (1, 1), (1, 2), (2, 2)])
    inputs_wait(2)
    e_wait(across, 4, low)
    e_wait(across, 5, high)
    gradient(across)
    inner_products([across, y, right, left], [(0, 0), (0, 1), (0, 2), (0, 3)])

    gsum[...] = jnp.zeros_like(gsum)
    ones = jnp.ones((8, 128), F32)
    lane = lax.broadcasted_iota(jnp.int32, (8, 128), 1)

    def to_lanes(sums):
        for p, value in enumerate(sums):
            gsum[p:p + 1, :] = jnp.sum(value, axis=0, keepdims=True)
        return lax.dot_general(
            ones, gsum[...], (((1,), (1,)), ((), ())), precision=lax.Precision.HIGHEST, preferred_element_type=F32
        )[0:1, :]

    def reduce_stage(value, slot, buffer, me, peers_of):
        mine[slot] = value
        buffer[me] = value
        for peer in peers_of:
            remote(mine.at[slot], buffer.at[me], r_send.at[slot], r_recv.at[slot], peer).start()
        count = len(peers_of)
        some = buffer.at[0:count]
        remote(some, some, r_send.at[slot], r_recv.at[slot], peers_of[0]).wait()
        total = buffer[0]
        for k in range(1, count + 1):
            total = total + buffer[k]
        return total

    def pick(vec, count):
        return [
            jnp.sum(jnp.where(lane[0:1] == p, vec, 0.0), axis=1, keepdims=True) for p in range(count)
        ]

    vec = to_lanes([gacc[a * NY + b] for a, b in YPAIRS])
    vec = reduce_stage(vec, 0, red.at[0], y * NT + t, plane)
    weights, _, _ = tree(pick(vec, len(YPAIRS)), YPAIRS)
    weights = [v * (1.0 / math.sqrt(rows)) for v in weights]

    def combine(b):
        lanes = pl.ds(pl.multiple_of(b * block, block), block)
        total = weights[0] * gbuf[0, :, lanes]
        for k in range(1, NY):
            total = total + weights[k] * gbuf[k, :, lanes]
        return total.astype(BF16)

    z_copies = []
    for k in (4, 3, 5, 2, 6, 1, 7):
        b = (z + k) % NZ
        zsend[k - 1] = combine(b)
        copy = remote(zsend.at[k - 1], zrecv.at[z], z_send.at[k - 1], z_recv.at[NZ - 1 - k], at(dz=k))
        copy.start()
        z_copies.append(copy)
    zrecv[z] = combine(z)

    q_copies = []

    def send_block(src, dst, sem, dx):
        copy = remote(src, dst, q_send.at[sem], q_recv.at[sem], at_x(dx, c))
        copy.start()
        q_copies.append(copy)

    send_block(ppart.at[2, low], qin.at[0], 0, 1)
    send_block(ppart.at[2, high], qin.at[1], 1, 3)
    send_block(ppart.at[1, high], xrecv.at[0, high], 2, 1)
    send_block(ppart.at[3, low], xrecv.at[1, low], 3, 3)
    for k in (1, 2, 3):
        ref = gin.at[(y + k) % NY, my_rows]
        remote(ref, ref, iy_send.at[k - 1], iy_recv.at[k - 1], at(dy=k)).wait_send()
    for copy in e_copies + copies + p_copies:
        copy.wait_send()
    q_copies[0].wait_recv()
    ppart[1, 0:half] = (ppart[1, 0:half].astype(F32) + qin[0].astype(F32)).astype(BF16)
    send_block(ppart.at[1, low], xrecv.at[0, low], 4, 1)
    q_copies[1].wait_recv()
    ppart[3, half:] = (ppart[3, half:].astype(F32) + qin[1].astype(F32)).astype(BF16)
    send_block(ppart.at[3, high], xrecv.at[1, high], 5, 3)
    for copy in q_copies[2:]:
        copy.wait_recv()
    ig[...] = (ppart[0].astype(F32) + (xrecv[0].astype(F32) + xrecv[1].astype(F32))).astype(BF16)
    ig_copy = pltpu.make_async_copy(ig, ig_out, out_sem.at[0])
    ig_copy.start()
    for copy in q_copies:
        copy.wait_send()

    def z_wait(k):
        ref = zrecv.at[(z + k) % NZ]
        remote(ref, ref, z_send.at[k - 1], z_recv.at[k - 1], at(dz=1)).wait_recv()

    def z_products(items, pairs):
        def step(i, sums):
            at_rows = pl.ds(pl.multiple_of(i * 16, 16), 16)
            values = [zrecv[k, at_rows, :].astype(F32) for k in items]
            out = []
            for s, (a, b) in zip(sums, pairs):
                product = values[a] * values[b]
                out.append(s + (product[0:8] + product[8:16]))
            return tuple(out)

        sums = lax.fori_loop(0, cols // 16, step, (zero,) * len(pairs), unroll=2)
        for value, (a, b) in zip(sums, pairs):
            low_index, high_index = jnp.minimum(items[a], items[b]), jnp.maximum(items[a], items[b])
            zacc[low_index * NZ + high_index] = value

    late, early = (7, 1), (4, 3, 5, 2, 6)
    for k in early:
        z_wait(k)
    items = [(z + k) % NZ for k in late + early + (0,)]
    z_products(items[2:], [(a, b) for a in range(6) for b in range(a, 6)])
    for k in late:
        z_wait(k)
    z_products(items, [(a, b) for a in range(2) for b in range(a, NZ)])
    vec = to_lanes([zacc[a * NZ + b] for a, b in ZPAIRS])
    vec = reduce_stage(vec, 1, zred, z, line)
    vec = reduce_stage(vec, 2, red.at[1], y * NT + t, plane)
    weights, first_sq, second_sq = tree(pick(vec, len(ZPAIRS)), ZPAIRS)
    total = weights[0] * zrecv[0].astype(F32)
    for k in range(1, NZ):
        total = total + weights[k] * zrecv[k].astype(F32)
    comb_out[...] = jnp.transpose(total)
    norm_out[...] = jnp.where(lane[0:1] == 0, jnp.sqrt(first_sq), jnp.sqrt(second_sq)) * (1.0 / width)
    for copy in z_copies:
        copy.wait_send()
    ig_copy.wait()


def finish(ig, comb, norm, momentum, ig_out, momentum_out, norm_out):
    ig_out[...] = ig[...]
    momentum_out[...] = 0.9 * momentum[...] + comb[...]
    norm_out[...] = norm[0, 0:2]


def body(inputs, weight, targets, momentum):
    rows, width = inputs.shape
    cols = weight.shape[1]
    block = width // (NZ * NY)
    wide = block * NZ
    dma = pltpu.SemaphoreType.DMA
    any_spec = pl.BlockSpec(memory_space=pl.ANY)
    vmem = pl.BlockSpec(memory_space=pltpu.VMEM)
    summed, combined, norms = pl.pallas_call(
        kernel,
        out_shape=(
            jax.ShapeDtypeStruct((cols, rows), BF16),
            jax.ShapeDtypeStruct((block, cols), F32),
            jax.ShapeDtypeStruct((1, 128), F32),
        ),
        in_specs=[any_spec] * 3,
        out_specs=(any_spec, vmem, vmem),
        scratch_shapes=[
            pltpu.VMEM((cols, rows), BF16),
            pltpu.VMEM((block, cols), F32),
            pltpu.VMEM((1, 128), F32),
            pltpu.VMEM((NY * NY, 8, 128), F32),
            pltpu.VMEM((NZ * NZ, 8, 128), F32),
            pltpu.VMEM((rows, width), BF16),
            pltpu.VMEM((width, cols), BF16),
            pltpu.VMEM((rows, cols), BF16),
            pltpu.VMEM((rows, cols), F32),
            pltpu.VMEM((NY, rows, wide), BF16),
            pltpu.VMEM((NY, cols, rows), BF16),
            pltpu.VMEM((NX, cols, rows), BF16),
            pltpu.VMEM((NX, cols, rows), BF16),
            pltpu.VMEM((NX, cols, rows), BF16),
            pltpu.VMEM((2, cols // 2, rows), BF16),
            pltpu.VMEM((2, cols, rows), BF16),
            pltpu.VMEM((NY, cols, wide), F32),
            pltpu.VMEM((NZ - 1, cols, block), BF16),
            pltpu.VMEM((NZ, cols, block), BF16),
            pltpu.VMEM((128, 128), F32),
            pltpu.VMEM((2, NY * NT, 1, 128), F32),
            pltpu.VMEM((NZ, 1, 128), F32),
            pltpu.VMEM((3, 1, 128), F32),
            dma((2 * KCHUNKS + 1,)),
            dma((3,)),
            dma,
            dma((3,)), dma((3,)),
            dma((18,)), dma((18,)),
            dma((12,)), dma((12,)),
            dma((6,)), dma((6,)),
            dma((NX,)), dma((NX,)),
            dma((6,)), dma((6,)),
            dma((NZ - 1,)), dma((NZ - 1,)),
            dma((3,)), dma((3,)),
        ],
        compiler_params=pltpu.CompilerParams(
            collective_id=0, has_side_effects=True, vmem_limit_bytes=53 * 2**20
        ),
    )(inputs, weight, targets)
    return pl.pallas_call(
        finish,
        out_shape=(
            jax.ShapeDtypeStruct((cols, rows), BF16),
            jax.ShapeDtypeStruct((block, cols), F32),
            jax.ShapeDtypeStruct((2,), F32),
        ),
        in_specs=[vmem, vmem, vmem, vmem],
        out_specs=(vmem, vmem, vmem),
        compiler_params=pltpu.CompilerParams(vmem_limit_bytes=4 * 2**20),
    )(summed, combined, norms, momentum)


def solution(mesh):
    return jax.shard_map(
        body,
        mesh=mesh,
        in_specs=(P("dp", None), P(None, "tensor"), P("dp", "tensor"), P("dp", "tensor")),
        out_specs=(P("tensor", "dp"), P("dp", "tensor"), P()),
        check_vma=False,
    )
```

```python
import functools
import math

import jax
import jax.numpy as jnp
from jax import lax
from jax.experimental import pallas as pl
from jax.experimental.pallas import tpu as pltpu
from jax.sharding import PartitionSpec as P

MESH = pl.DeviceIdType.MESH
NZ, NY, NX, NC = 8, 4, 4, 2
NT = NX * NC
F32, BF16 = jnp.float32, jnp.bfloat16
KCHUNKS = 4
YPAIRS = [(i, j) for i in range(NY) for j in range(i, NY)]
ZPAIRS = [(i, j) for i in range(NZ) for j in range(i, NZ)]


def tree(gram, pairs):
    count = max(j for _, j in pairs) + 1
    value = {}
    for at, (i, j) in enumerate(pairs):
        value[i, j] = value[j, i] = gram[at]
    items = [{i: None} for i in range(count)]

    def weighted(term, coefficient):
        return term if coefficient is None else term * coefficient

    def inner(first, second):
        total = None
        for i, a in first.items():
            for j, c in second.items():
                term = weighted(weighted(value[i, j], a), c)
                total = term if total is None else total + term
        return total

    while len(items) > 1:
        merged = []
        for at in range(0, len(items), 2):
            first, second = items[at], items[at + 1]
            cross, first_sq, second_sq = inner(first, second), inner(first, first), inner(second, second)
            left = 1.0 - cross / (2.0 * first_sq)
            right = 1.0 - cross / (2.0 * second_sq)
            item = {i: weighted(left, a) for i, a in first.items()}
            item.update({i: weighted(right, c) for i, c in second.items()})
            merged.append(item)
        items = merged
    return [items[0][i] for i in range(count)], first_sq, second_sq


def kernel(
    inputs, weight, targets,
    ig_out, comb_out, norm_out,
    ig, comb, norm, gacc, zacc,
    xin, w, tg, acc, gin, et, psend, precv, ppart, qin, xrecv, gbuf, zsend, zrecv,
    gsum, red, zred, mine,
    ld_sem, out_sem, own_sem, iy_send, iy_recv, ix_send, ix_recv, is_send, is_recv,
    e_send, e_recv, p_send, p_recv, q_send, q_recv, z_send, z_recv, r_send, r_recv,
):
    dp, t = lax.axis_index("dp"), lax.axis_index("tensor")
    z, y, x, c = dp // NY, dp % NY, t // NC, t % NC
    rows, width = inputs.shape
    cols = weight.shape[1]
    kc = width // KCHUNKS
    part_rows = rows // NT
    block = width // (NZ * NY)
    wide = block * NZ

    def at(dz=0, dy=0, dt=None):
        return ((z + dz) % NZ * NY + (y + dy) % NY, t if dt is None else (t + dt) % NT)

    def at_x(dx, core):
        return (dp, (x + dx) % NX * NC + core)

    barrier = pltpu.get_barrier_semaphore()
    line = [at(dz=k) for k in (4, 3, 5, 2, 6, 1, 7)]
    plane = [
        (z * NY + (y + dy) % NY, (x + dx) % NX * NC + (c + dc) % NC)
        for dx in (2, 1, 3, 0) for dy in (2, 1, 3, 0) for dc in range(NC) if dx or dy or dc
    ]
    peers = line + plane
    for peer in peers:
        pl.semaphore_signal(barrier, inc=1, device_id=peer, device_id_type=MESH)
    loads = []
    for i in range(KCHUNKS):
        a = pltpu.make_async_copy(inputs.at[:, i * kc:(i + 1) * kc], xin.at[:, i * kc:(i + 1) * kc], ld_sem.at[2 * i])
        b = pltpu.make_async_copy(weight.at[i * kc:(i + 1) * kc], w.at[i * kc:(i + 1) * kc], ld_sem.at[2 * i + 1])
        a.start()
        b.start()
        loads.append((a, b))
    tg_load = pltpu.make_async_copy(targets, tg, ld_sem.at[2 * KCHUNKS])
    tg_load.start()

    pl.semaphore_wait(barrier, len(peers))

    def remote(src, dst, send, recv, peer):
        return pltpu.make_async_remote_copy(
            src_ref=src, dst_ref=dst, send_sem=send, recv_sem=recv, device_id=peer, device_id_type=MESH
        )

    my_rows = pl.ds(pl.multiple_of(t * part_rows, part_rows), part_rows)
    for k in (1, 3, 2):
        for b in range(NZ):
            col = pl.multiple_of((b * NY + (y + k) % NY) * block, block)
            remote(
                inputs.at[my_rows, pl.ds(col, block)], gin.at[y, my_rows, b * block:(b + 1) * block],
                iy_send.at[k - 1], iy_recv.at[3 - k], at(dy=k),
            ).start()
    for b in range(NZ):
        col = pl.multiple_of((b * NY + y) * block, block)
        pltpu.make_async_copy(inputs.at[:, pl.ds(col, block)], gin.at[y, :, b * block:(b + 1) * block], own_sem).start()

    for i, (a, b) in enumerate(loads):
        a.wait()
        b.wait()
        part = jnp.dot(xin[:, i * kc:(i + 1) * kc], w[i * kc:(i + 1) * kc, :], preferred_element_type=F32)
        if i == 0:
            acc[...] = part
        else:
            acc[...] += part
    tg_load.wait()
    et[y] = jnp.transpose((acc[...] - tg[...].astype(F32)).astype(BF16))

    half = cols // 2
    low, high = pl.ds(0, half), pl.ds(half, half)
    right, left, across = (y + 1) % NY, (y + 3) % NY, (y + 2) % NY

    def send_error(index, sem, part, dy):
        copy = remote(et.at[index, part], et.at[index, part], e_send.at[sem], e_recv.at[sem], at(dy=dy))
        copy.start()
        return copy

    e_copies = [
        send_error(y, 0, low, 3),
        send_error(y, 3, high, 1),
        send_error(y, 1, high, 3),
        send_error(y, 2, low, 1),
    ]

    def e_wait(index, sem, part):
        remote(et.at[index, part], et.at[index, part], e_send.at[sem], e_recv.at[sem], at(dy=1)).wait_recv()

    sib = at_x(0, 1 - c)
    def rows_of(dx, core):
        return pl.multiple_of(((x + dx) % NX * NC + core) * part_rows, part_rows)

    sub = part_rows // 2
    copies = []

    def share(k, start, count, sends, recvs, sem, peer):
        ref = gin.at[(y + k) % NY, pl.ds(start, count)]
        copy = remote(ref, ref, sends.at[sem], recvs.at[sem], peer)
        copy.start()
        copies.append(copy)

    def shared(k, start, count, sends, recvs, sem):
        ref = gin.at[(y + k) % NY, pl.ds(start, count)]
        remote(ref, ref, sends.at[sem], recvs.at[sem], sib).wait_recv()

    mine_low = rows_of(0, c)
    mine_high = mine_low + sub
    right_low = rows_of(1, c)
    left_low = rows_of(3, c)
    across_low = rows_of(2, c)
    order = (1, 3, 2)
    for k in order:
        ref = gin.at[(y + k) % NY, my_rows]
        remote(ref, ref, iy_send.at[k - 1], iy_recv.at[k - 1], at(dy=k)).wait_recv()
        share(k, mine_low, sub, ix_send, ix_recv, k - 1, at_x(3, c))
        share(k, mine_high, sub, ix_send, ix_recv, 6 + k - 1, at_x(1, c))
        share(k, mine_high, sub, ix_send, ix_recv, 3 + k - 1, at_x(3, c))
        share(k, mine_low, sub, ix_send, ix_recv, 9 + k - 1, at_x(1, c))
        share(k, mine_low, part_rows, is_send, is_recv, k - 1, sib)

    p_copies = []
    for j in range(NX):
        start = pl.multiple_of(((x + j) % NX * NC + 1 - c) * cols, cols)
        psend[j] = jnp.dot(w[pl.ds(start, cols), :], et[y], preferred_element_type=F32).astype(BF16)
        copy = remote(psend.at[j], precv.at[j], p_send.at[j], p_recv.at[j], sib)
        copy.start()
        p_copies.append(copy)
    for j in range(NX):
        start = pl.multiple_of(((x + j) % NX * NC + c) * cols, cols)
        ppart[j] = jnp.dot(w[pl.ds(start, cols), :], et[y], preferred_element_type=F32).astype(BF16)

    def gradient(index):
        gbuf[index] = jnp.dot(et[index], gin[index], preferred_element_type=F32)

    pltpu.make_async_copy(gin.at[y], gin.at[y], own_sem).wait()
    gradient(y)

    for k in order:
        shared(k, right_low, sub, ix_send, ix_recv, k - 1)
        share(k, right_low, sub, ix_send, ix_recv, 12 + k - 1, at_x(3, c))
        shared(k, left_low + sub, sub, ix_send, ix_recv, 6 + k - 1)
        share(k, left_low + sub, sub, ix_send, ix_recv, 15 + k - 1, at_x(1, c))
    e_wait(right, 0, low)
    e_copies.append(send_error(right, 4, low, 3))
    e_wait(left, 3, high)
    e_copies.append(send_error(left, 5, high, 1))
    for j in range(NX):
        p_copies[j].wait_recv()
        ppart[j] = (ppart[j].astype(F32) + precv[j].astype(F32)).astype(BF16)
    for k in order:
        shared(k, right_low + sub, sub, ix_send, ix_recv, 3 + k - 1)
        share(k, right_low, part_rows, is_send, is_recv, 3 + k - 1, sib)
        shared(k, left_low, sub, ix_send, ix_recv, 9 + k - 1)
        share(k, left_low, part_rows, is_send, is_recv, 6 + k - 1, sib)
    for k in order:
        shared(k, across_low, sub, ix_send, ix_recv, 12 + k - 1)
        shared(k, across_low + sub, sub, ix_send, ix_recv, 15 + k - 1)
        share(k, across_low, part_rows, is_send, is_recv, 9 + k - 1, sib)

    def inputs_wait(k):
        for n, dx in enumerate((0, 1, 3, 2)):
            shared(k, rows_of(dx, 1 - c), part_rows, is_send, is_recv, 3 * n + k - 1)

    def fold(value):
        total = value[:, 0:128]
        for l in range(1, value.shape[1] // 128):
            total = total + value[:, l * 128:(l + 1) * 128]
        return total

    zero = jnp.zeros((8, 128), F32)

    def inner_products(items, pairs):
        def step(i, sums):
            at_rows = pl.ds(pl.multiple_of(i * 8, 8), 8)
            values = [gbuf[k, at_rows, :] for k in items]
            return tuple(s + fold(values[a] * values[b]) for s, (a, b) in zip(sums, pairs))

        sums = lax.fori_loop(0, cols // 8, step, (zero,) * len(pairs), unroll=4)
        for value, (a, b) in zip(sums, pairs):
            low_index, high_index = jnp.minimum(items[a], items[b]), jnp.maximum(items[a], items[b])
            gacc[low_index * NY + high_index] = value

    e_wait(right, 1, high)
    inputs_wait(1)
    gradient(right)
    e_wait(left, 2, low)
    inputs_wait(3)
    gradient(left)
    inner_products([y, right, left], [(0, 0), (0, 1), (0, 2), (1, 1), (1, 2), (2, 2)])
    inputs_wait(2)
    e_wait(across, 4, low)
    e_wait(across, 5, high)
    gradient(across)
    inner_products([across, y, right, left], [(0, 0), (0, 1), (0, 2), (0, 3)])

    gsum[...] = jnp.zeros_like(gsum)
    ones = jnp.ones((8, 128), F32)
    lane = lax.broadcasted_iota(jnp.int32, (8, 128), 1)

    def to_lanes(sums):
        for p, value in enumerate(sums):
            gsum[p:p + 1, :] = jnp.sum(value, axis=0, keepdims=True)
        return lax.dot_general(
            ones, gsum[...], (((1,), (1,)), ((), ())), precision=lax.Precision.HIGHEST, preferred_element_type=F32
        )[0:1, :]

    def reduce_stage(value, slot, buffer, me, peers_of):
        mine[slot] = value
        buffer[me] = value
        for peer in peers_of:
            remote(mine.at[slot], buffer.at[me], r_send.at[slot], r_recv.at[slot], peer).start()
        count = len(peers_of)
        some = buffer.at[0:count]
        remote(some, some, r_send.at[slot], r_recv.at[slot], peers_of[0]).wait()
        total = buffer[0]
        for k in range(1, count + 1):
            total = total + buffer[k]
        return total

    def pick(vec, count):
        return [
            jnp.sum(jnp.where(lane[0:1] == p, vec, 0.0), axis=1, keepdims=True) for p in range(count)
        ]

    vec = to_lanes([gacc[a * NY + b] for a, b in YPAIRS])
    vec = reduce_stage(vec, 0, red.at[0], y * NT + t, plane)
    weights, _, _ = tree(pick(vec, len(YPAIRS)), YPAIRS)
    weights = [v * (1.0 / math.sqrt(rows)) for v in weights]

    def combine(b):
        lanes = pl.ds(pl.multiple_of(b * block, block), block)
        total = weights[0] * gbuf[0, :, lanes]
        for k in range(1, NY):
            total = total + weights[k] * gbuf[k, :, lanes]
        return total.astype(BF16)

    z_copies = []
    for k in (4, 3, 5, 2, 6, 1, 7):
        b = (z + k) % NZ
        zsend[k - 1] = combine(b)
        copy = remote(zsend.at[k - 1], zrecv.at[z], z_send.at[k - 1], z_recv.at[NZ - 1 - k], at(dz=k))
        copy.start()
        z_copies.append(copy)
    zrecv[z] = combine(z)

    q_copies = []

    def send_block(src, dst, sem, dx):
        copy = remote(src, dst, q_send.at[sem], q_recv.at[sem], at_x(dx, c))
        copy.start()
        q_copies.append(copy)

    send_block(ppart.at[2, low], qin.at[0], 0, 1)
    send_block(ppart.at[2, high], qin.at[1], 1, 3)
    send_block(ppart.at[1, high], xrecv.at[0, high], 2, 1)
    send_block(ppart.at[3, low], xrecv.at[1, low], 3, 3)
    for k in (1, 2, 3):
        ref = gin.at[(y + k) % NY, my_rows]
        remote(ref, ref, iy_send.at[k - 1], iy_recv.at[k - 1], at(dy=k)).wait_send()
    for copy in e_copies + copies + p_copies:
        copy.wait_send()
    q_copies[0].wait_recv()
    ppart[1, 0:half] = (ppart[1, 0:half].astype(F32) + qin[0].astype(F32)).astype(BF16)
    send_block(ppart.at[1, low], xrecv.at[0, low], 4, 1)
    q_copies[1].wait_recv()
    ppart[3, half:] = (ppart[3, half:].astype(F32) + qin[1].astype(F32)).astype(BF16)
    send_block(ppart.at[3, high], xrecv.at[1, high], 5, 3)
    for copy in q_copies[2:]:
        copy.wait_recv()
    ig[...] = (ppart[0].astype(F32) + (xrecv[0].astype(F32) + xrecv[1].astype(F32))).astype(BF16)
    ig_copy = pltpu.make_async_copy(ig, ig_out, out_sem.at[0])
    ig_copy.start()
    for copy in q_copies:
        copy.wait_send()

    def z_wait(k):
        ref = zrecv.at[(z + k) % NZ]
        remote(ref, ref, z_send.at[k - 1], z_recv.at[k - 1], at(dz=1)).wait_recv()

    def z_products(items, pairs):
        def step(i, sums):
            at_rows = pl.ds(pl.multiple_of(i * 16, 16), 16)
            values = [zrecv[k, at_rows, :].astype(F32) for k in items]
            out = []
            for s, (a, b) in zip(sums, pairs):
                product = values[a] * values[b]
                out.append(s + (product[0:8] + product[8:16]))
            return tuple(out)

        sums = lax.fori_loop(0, cols // 16, step, (zero,) * len(pairs), unroll=4)
        for value, (a, b) in zip(sums, pairs):
            low_index, high_index = jnp.minimum(items[a], items[b]), jnp.maximum(items[a], items[b])
            zacc[low_index * NZ + high_index] = value

    late, early = (7, 1), (4, 3, 5, 2, 6)
    for k in early:
        z_wait(k)
    items = [(z + k) % NZ for k in late + early + (0,)]
    z_products(items[2:], [(a, b) for a in range(6) for b in range(a, 6)])
    for k in late:
        z_wait(k)
    z_products(items, [(a, b) for a in range(2) for b in range(a, NZ)])
    vec = to_lanes([zacc[a * NZ + b] for a, b in ZPAIRS])
    vec = reduce_stage(vec, 1, zred, z, line)
    vec = reduce_stage(vec, 2, red.at[1], y * NT + t, plane)
    weights, first_sq, second_sq = tree(pick(vec, len(ZPAIRS)), ZPAIRS)
    total = weights[0] * zrecv[0].astype(F32)
    for k in range(1, NZ):
        total = total + weights[k] * zrecv[k].astype(F32)
    comb_out[...] = jnp.transpose(total)
    norm_out[...] = jnp.where(lane[0:1] == 0, jnp.sqrt(first_sq), jnp.sqrt(second_sq)) * (1.0 / width)
    for copy in z_copies:
        copy.wait_send()
    ig_copy.wait()


def finish(ig, comb, norm, momentum, ig_out, momentum_out, norm_out):
    ig_out[...] = ig[...]
    momentum_out[...] = 0.9 * momentum[...] + comb[...]
    norm_out[...] = norm[0, 0:2]


def body(inputs, weight, targets, momentum):
    rows, width = inputs.shape
    cols = weight.shape[1]
    block = width // (NZ * NY)
    wide = block * NZ
    dma = pltpu.SemaphoreType.DMA
    any_spec = pl.BlockSpec(memory_space=pl.ANY)
    vmem = pl.BlockSpec(memory_space=pltpu.VMEM)
    summed, combined, norms = pl.pallas_call(
        kernel,
        out_shape=(
            jax.ShapeDtypeStruct((cols, rows), BF16),
            jax.ShapeDtypeStruct((block, cols), F32),
            jax.ShapeDtypeStruct((1, 128), F32),
        ),
        in_specs=[any_spec] * 3,
        out_specs=(any_spec, vmem, vmem),
        scratch_shapes=[
            pltpu.VMEM((cols, rows), BF16),
            pltpu.VMEM((block, cols), F32),
            pltpu.VMEM((1, 128), F32),
            pltpu.VMEM((NY * NY, 8, 128), F32),
            pltpu.VMEM((NZ * NZ, 8, 128), F32),
            pltpu.VMEM((rows, width), BF16),
            pltpu.VMEM((width, cols), BF16),
            pltpu.VMEM((rows, cols), BF16),
            pltpu.VMEM((rows, cols), F32),
            pltpu.VMEM((NY, rows, wide), BF16),
            pltpu.VMEM((NY, cols, rows), BF16),
            pltpu.VMEM((NX, cols, rows), BF16),
            pltpu.VMEM((NX, cols, rows), BF16),
            pltpu.VMEM((NX, cols, rows), BF16),
            pltpu.VMEM((2, cols // 2, rows), BF16),
            pltpu.VMEM((2, cols, rows), BF16),
            pltpu.VMEM((NY, cols, wide), F32),
            pltpu.VMEM((NZ - 1, cols, block), BF16),
            pltpu.VMEM((NZ, cols, block), BF16),
            pltpu.VMEM((128, 128), F32),
            pltpu.VMEM((2, NY * NT, 1, 128), F32),
            pltpu.VMEM((NZ, 1, 128), F32),
            pltpu.VMEM((3, 1, 128), F32),
            dma((2 * KCHUNKS + 1,)),
            dma((3,)),
            dma,
            dma((3,)), dma((3,)),
            dma((18,)), dma((18,)),
            dma((12,)), dma((12,)),
            dma((6,)), dma((6,)),
            dma((NX,)), dma((NX,)),
            dma((6,)), dma((6,)),
            dma((NZ - 1,)), dma((NZ - 1,)),
            dma((3,)), dma((3,)),
        ],
        compiler_params=pltpu.CompilerParams(
            collective_id=0, has_side_effects=True, vmem_limit_bytes=53 * 2**20
        ),
    )(inputs, weight, targets)
    return pl.pallas_call(
        finish,
        out_shape=(
            jax.ShapeDtypeStruct((cols, rows), BF16),
            jax.ShapeDtypeStruct((block, cols), F32),
            jax.ShapeDtypeStruct((2,), F32),
        ),
        in_specs=[vmem, vmem, vmem, vmem],
        out_specs=(vmem, vmem, vmem),
        compiler_params=pltpu.CompilerParams(vmem_limit_bytes=4 * 2**20),
    )(summed, combined, norms, momentum)


def solution(mesh):
    return jax.shard_map(
        body,
        mesh=mesh,
        in_specs=(P("dp", None), P(None, "tensor"), P("dp", "tensor"), P("dp", "tensor")),
        out_specs=(P("tensor", "dp"), P("dp", "tensor"), P()),
        check_vma=False,
    )
```
